32 devices in a mesh: groups: 2 (over y), blk: 4 (over z), rep: 2 (over x), sub: 2 (over core).
Axes of the slice: x: 2, y: 2, z: 4, core: 2. Of those that a mesh axis runs over, the one named last changes fastest.
Arguments:
- positions: float32 [3, 12288], P(None, ('groups', 'blk', 'rep', 'sub')), parts along dimension 1, may hold values from -19 to 19
- velocities: float32 [3, 12288], P(None, ('groups', 'blk', 'rep', 'sub')), parts along dimension 1, may hold values from -6 to 6
- charges: float32 [12288], P(('groups', 'blk', 'rep', 'sub')), parts along dimension 0, may hold values from -2.4 to 2.4
- dipoles: float32 [3, 12288], P(None, ('groups', 'blk', 'rep', 'sub')), parts along dimension 1, may hold values from -1.8 to 1.8
- quadrupoles: float32 [6, 12288], P(None, ('groups', 'blk', 'rep', 'sub')), parts along dimension 1, may hold values from -1.2 to 1.2
- damping: float32 [12288], P(('groups', 'blk', 'rep', 'sub')), parts along dimension 0, may hold values from 0.5 to 2
- inverse_mass: float32 [12288], P(('groups', 'blk', 'rep', 'sub')), parts along dimension 0, may hold values from 0.0625 to 1
- bonds: int32 [2, 12288], P(None, ('groups', 'blk', 'rep', 'sub')), parts along dimension 1, may hold values from 0 to 767
- bond_length: float32 [12288], P(('groups', 'blk', 'rep', 'sub')), parts along dimension 0, may hold values from 1 to 4
- angles: int32 [3, 24576], P(None, ('groups', 'blk', 'rep', 'sub')), parts along dimension 1, may hold values from 0 to 767
- torsions: int32 [4, 24576], P(None, ('groups', 'blk', 'rep', 'sub')), parts along dimension 1, may hold values from 0 to 767
Outputs:
- new_positions: float32 [3, 12288], P(None, ('groups', 'blk', 'rep', 'sub')), parts along dimension 1
- new_velocities: float32 [3, 12288], P(None, ('groups', 'blk', 'rep', 'sub')), parts along dimension 1
- slow_force: float32 [3, 12288], P(None, ('groups', 'blk', 'rep', 'sub')), parts along dimension 1
- slow_torque: float32 [3, 12288], P(None, ('groups', 'blk', 'rep', 'sub')), parts along dimension 1
The draws below stay inside these ranges and needn't reach their ends.
There are 2 independent parts, one for each index of `groups`. The reference program is written for one: setup_inputs(seed, part) draws one part's arguments, and reference() takes and returns one part's arrays. A program takes and returns all parts, laid end to end along the dimension named above; each array names one. Nothing has to cross between parts.
Inputs may be any that keep to these rules, and one draw needn't show every extreme that they name: `bonds`: bond term k indexes atoms of domain k // 768, counted within it. `angles`: angle term k indexes atoms of domain k // 1536, counted within it. `torsions`: torsion term k indexes atoms of domain k // 1536, counted within it.
All inputs are finite; a program needn't handle non-finite values.
Results may differ from the reference program's by a relative error of at most 0.0003.
Values sent between devices are 32-bit elements; how exact they have to be, the bound alone decides.
A program may use at most 64 MiB of HBM per device.

```python
import math
import jax
import jax.numpy as jnp
from jax import lax

ATOM_DEV = 384
INNER = 4
ATOMS = 6144
DOMAIN_ATOMS = 768
BONDS = 6144
ANGLES = 12288
TORSIONS = 12288


def draw_positions(key, part):
    key_centre = jax.random.fold_in(key, 11)
    key_offset = jax.random.fold_in(key, 12)
    centres = jax.random.uniform(key_centre, (3, ATOMS // DOMAIN_ATOMS), jnp.float32, -10.0, 10.0)
    offsets = jnp.clip(3.0 * jax.random.normal(key_offset, (3, ATOMS), jnp.float32), -9.0, 9.0)
    return jnp.repeat(centres, DOMAIN_ATOMS, axis=1) + offsets


def with_ends(drawn, rng, smallest, top_value):
    longest = drawn.shape.index(max(drawn.shape))
    spots = []
    for shift in (0, 1):
        where = [jax.random.randint(jax.random.fold_in(rng, axis), (), 0, length) for axis, length in enumerate(drawn.shape)]
        where[longest] = (where[longest] + shift) % drawn.shape[longest]
        spots.append(tuple(where))
    return drawn.at[spots[0]].set(smallest).at[spots[1]].set(top_value)


def level_of(rng, shape, pieces, low, high):
    def one(axis_at, blocks):
        draws = jax.random.uniform(jax.random.fold_in(jax.random.fold_in(rng, 6), axis_at), (blocks,), jnp.float32, low / len(pieces), high / len(pieces))
        return jnp.repeat(jnp.exp(draws), shape[axis_at] // blocks).reshape((-1,) + (1,) * (len(shape) - axis_at - 1))

    loudness = one(*pieces[0])
    for cut in pieces[1:]:
        loudness = loudness * one(*cut)
    return loudness


def noise(own_key, shape, deviation, reach, cuts=(), kind=jnp.bfloat16):
    entries = jax.random.normal(own_key, shape, jnp.float32) * deviation
    if len(cuts) > 0:
        entries = level_of(own_key, shape, cuts, -0.22, 0.18) * entries
    return jnp.clip(entries, min=-reach, max=reach).astype(kind)


def setup_inputs(seed: int = 0, part: int = 0) -> dict:
    streams_of = jax.random.split(jax.random.key(seed), 12)
    part_keys = jax.random.split(jax.random.fold_in(streams_of[11], part), 12)
    positions = draw_positions(jax.random.fold_in(jax.random.fold_in(streams_of[11], part), 71), part)
    velocities = noise(part_keys[1], (3, ATOMS), 1.0, 6.0, ((1, 16),), jnp.float32)
    charges = noise(part_keys[2], (ATOMS,), 0.4, 2.4, ((0, 16),), jnp.float32)
    dipoles = noise(part_keys[3], (3, ATOMS), 0.3, 1.8, ((1, 16),), jnp.float32)
    quadrupoles = noise(part_keys[4], (6, ATOMS), 0.2, 1.2, ((1, 16),), jnp.float32)
    damping = jnp.clip(jnp.exp(math.log(2.0) - 1.3862944 * jax.random.uniform(part_keys[5], (ATOMS,), jnp.float32) ** level_of(part_keys[5], (ATOMS,), ((0, 16),), -0.2, 0.2)), 0.5, 2.0)
    inverse_mass = jnp.clip(jnp.exp(math.log(1.0) - 2.7725887 * jax.random.uniform(part_keys[6], (ATOMS,), jnp.float32) ** level_of(part_keys[6], (ATOMS,), ((0, 16),), -0.2, 0.2)), 0.0625, 1.0)
    bonds = with_ends(jax.random.randint(part_keys[7], (2, BONDS), 0, DOMAIN_ATOMS), jax.random.fold_in(part_keys[7], 1), 0, DOMAIN_ATOMS - 1).astype(jnp.int32)
    bond_length = jnp.clip(1.0 + 3.0 * jax.random.uniform(part_keys[8], (BONDS,), jnp.float32) ** level_of(part_keys[8], (BONDS,), ((0, 16),), -0.2, 0.2), 1.0, 4.0)
    angles = with_ends(jax.random.randint(part_keys[9], (3, ANGLES), 0, DOMAIN_ATOMS), jax.random.fold_in(part_keys[9], 1), 0, DOMAIN_ATOMS - 1).astype(jnp.int32)
    torsions = with_ends(jax.random.randint(part_keys[10], (4, TORSIONS), 0, DOMAIN_ATOMS), jax.random.fold_in(part_keys[10], 1), 0, DOMAIN_ATOMS - 1).astype(jnp.int32)
    return dict(positions=positions, velocities=velocities, charges=charges, dipoles=dipoles, quadrupoles=quadrupoles, damping=damping, inverse_mass=inverse_mass, bonds=bonds, bond_length=bond_length, angles=angles, torsions=torsions)


QUAD_INDEX = ((0, 1, 2), (1, 3, 4), (2, 4, 5))
BOND_K = 0.3
ANGLE_K = 4.0
ANGLE_REST = -0.33
TORSION_K = 2.0
OUTER_DT = 0.2

def inner3(left, right):
    return left[0] * right[0] + left[1] * right[1] + left[2] * right[2]

def pair_energy(target_pos, target_dip, target_quad, target_charge, target_damp, source, target_ids, source_ids):
    separation = [source[c][None, :] - target_pos[c][:, None] for c in range(3)]
    dist_sq = inner3(separation, separation) + target_damp[:, None] * source[13][None, :]
    inv_one = lax.rsqrt(dist_sq)
    inv_three = inv_one / dist_sq
    inv_five = 3.0 * inv_three / dist_sq
    inv_seven = 5.0 * inv_five / dist_sq
    inv_nine = 7.0 * inv_seven / dist_sq
    charge_i = target_charge[:, None]
    charge_k = source[3][None, :]
    dip_i = [target_dip[c][:, None] for c in range(3)]
    dip_k = [source[4 + c][None, :] for c in range(3)]
    quad_i = [[target_quad[QUAD_INDEX[a][b]][:, None] for b in range(3)] for a in range(3)]
    quad_k = [[source[7 + QUAD_INDEX[a][b]][None, :] for b in range(3)] for a in range(3)]
    quad_ir = [inner3(quad_i[a], separation) for a in range(3)]
    quad_kr = [inner3(quad_k[a], separation) for a in range(3)]
    dip_ir = inner3(dip_i, separation)
    dip_kr = inner3(dip_k, separation)
    dip_ik = inner3(dip_i, dip_k)
    quad_rri = inner3(quad_ir, separation)
    quad_rrk = inner3(quad_kr, separation)
    quad_rrik = inner3(quad_ir, quad_kr)
    quad_ik = sum((quad_i[a][b] * quad_k[a][b] for a in range(3) for b in range(3)))
    dip_iqk = inner3(dip_i, quad_kr)
    dip_kqi = inner3(dip_k, quad_ir)
    term_one = charge_i * charge_k
    term_two = charge_k * dip_ir - charge_i * dip_kr + dip_ik
    term_three = charge_i * quad_rrk + charge_k * quad_rri - dip_ir * dip_kr + 2.0 * (dip_kqi - dip_iqk + quad_ik)
    term_four = dip_ir * quad_rrk - dip_kr * quad_rri - 4.0 * quad_rrik
    term_five = quad_rri * quad_rrk
    energy = term_one * inv_one + term_two * inv_three + term_three * inv_five + term_four * inv_seven + term_five * inv_nine
    distinct = target_ids[:, None] != source_ids[None, :]
    return jnp.sum(jnp.where(distinct, energy, 0.0))

def pair_gradients(target, source, target_ids, source_ids):

    def tile_energy(target_pos, target_dip, target_quad):
        return pair_energy(target_pos, target_dip, target_quad, target[3], target[13], source, target_ids, source_ids)
    grads = jax.grad(tile_energy, argnums=(0, 1, 2))(target[0:3], target[4:7], target[7:13])
    return jnp.concatenate(grads, 0)

def finish(partials, dipoles, quadrupoles):
    slow_force = -partials[0:3]
    field_dip = -partials[3:6]
    grad_quad = partials[6:12]
    halves = (1.0, 0.5, 0.5, 1.0, 0.5, 1.0)
    grad_matrix = [[halves[QUAD_INDEX[a][b]] * grad_quad[QUAD_INDEX[a][b]] for b in range(3)] for a in range(3)]
    quad_matrix = [[quadrupoles[QUAD_INDEX[a][b]] for b in range(3)] for a in range(3)]
    product = [[quad_matrix[a][0] * grad_matrix[0][b] + quad_matrix[a][1] * grad_matrix[1][b] + quad_matrix[a][2] * grad_matrix[2][b] for b in range(3)] for a in range(3)]
    torque = jnp.stack([dipoles[1] * field_dip[2] - dipoles[2] * field_dip[1] - 2.0 * (product[1][2] - product[2][1]), dipoles[2] * field_dip[0] - dipoles[0] * field_dip[2] - 2.0 * (product[2][0] - product[0][2]), dipoles[0] * field_dip[1] - dipoles[1] * field_dip[0] - 2.0 * (product[0][1] - product[1][0])])
    return (slow_force, torque)

def bonded_energy(coords, bonds, bond_length, angles, torsions):

    def picked(rows):
        return coords[:, rows]
    stretch = picked(bonds[1]) - picked(bonds[0])
    length_now = jnp.sqrt(lax.optimization_barrier(jnp.sum(stretch * stretch, 0)) + 0.01)
    bond_gap = length_now - bond_length
    bond_part = 0.5 * BOND_K * jnp.sum(bond_gap * bond_gap)
    arm_first = picked(angles[0]) - picked(angles[1])
    arm_second = picked(angles[2]) - picked(angles[1])
    cosine = lax.optimization_barrier(jnp.sum(arm_first * arm_second, 0)) * lax.rsqrt((lax.optimization_barrier(jnp.sum(arm_first * arm_first, 0)) + 0.01) * (lax.optimization_barrier(jnp.sum(arm_second * arm_second, 0)) + 0.01))
    angle_gap = cosine - ANGLE_REST
    angle_part = 0.5 * ANGLE_K * jnp.sum(angle_gap * angle_gap)
    bond_one = picked(torsions[1]) - picked(torsions[0])
    bond_two = picked(torsions[2]) - picked(torsions[1])
    bond_three = picked(torsions[3]) - picked(torsions[2])
    normal_one = jnp.cross(bond_one, bond_two, axis=0)
    normal_two = jnp.cross(bond_two, bond_three, axis=0)
    dihedral = lax.optimization_barrier(jnp.sum(normal_one * normal_two, 0)) * lax.rsqrt((lax.optimization_barrier(jnp.sum(normal_one * normal_one, 0)) + 0.1) * (lax.optimization_barrier(jnp.sum(normal_two * normal_two, 0)) + 0.1))
    torsion_part = TORSION_K * jnp.sum(1.0 + dihedral)
    return bond_part + angle_part + torsion_part

def reference(positions, velocities, charges, dipoles, quadrupoles, damping, inverse_mass, bonds, bond_length, angles, torsions):
    record = jnp.concatenate([positions, charges[None, :], dipoles, quadrupoles, damping[None, :]], 0)
    atom_ids = jnp.arange(ATOMS, dtype=jnp.int32)
    target_width = ATOM_DEV
    source_width = 2 * ATOM_DEV
    target_blocks = record.reshape(14, ATOMS // target_width, target_width).transpose(1, 0, 2)
    target_idblk = atom_ids.reshape(ATOMS // target_width, target_width)
    source_blocks = record.reshape(14, ATOMS // source_width, source_width).transpose(1, 0, 2)
    source_idblk = atom_ids.reshape(ATOMS // source_width, source_width)

    def one_target(packed):
        target, target_ids = packed

        def add_source(summed, source_pack):
            source, source_ids = source_pack
            return (summed + pair_gradients(target, source, target_ids, source_ids), None)
        summed, _unused = lax.scan(add_source, jnp.zeros((12, target_width), jnp.float32), (source_blocks, source_idblk))
        return summed
    partials = lax.map(one_target, (target_blocks, target_idblk)).transpose(1, 0, 2).reshape(12, ATOMS)
    slow_force, slow_torque = finish(partials, dipoles, quadrupoles)
    bond_offset = jnp.arange(ATOMS, dtype=jnp.int32) // DOMAIN_ATOMS * DOMAIN_ATOMS
    term_offset = jnp.arange(2 * ATOMS, dtype=jnp.int32) // (2 * DOMAIN_ATOMS) * DOMAIN_ATOMS
    global_bonds = bonds + bond_offset[None, :]
    global_angles = angles + term_offset[None, :]
    global_torsions = torsions + term_offset[None, :]

    def bonded_push(coords):
        return -jax.grad(bonded_energy)(coords, global_bonds, bond_length, global_angles, global_torsions)
    inner_dt = OUTER_DT / INNER
    velocity = velocities + 0.5 * OUTER_DT * slow_force * inverse_mass[None, :]
    coords = positions
    push = bonded_push(coords)
    for substep in range(INNER):
        velocity = velocity + 0.5 * inner_dt * push * inverse_mass[None, :]
        coords = coords + inner_dt * velocity
        push = bonded_push(coords)
        velocity = velocity + 0.5 * inner_dt * push * inverse_mass[None, :]
    return (coords, velocity, slow_force, slow_torque)
```

```python
import functools

import jax
import jax.numpy as jnp
from jax import lax
from jax.experimental import pallas as pl
from jax.experimental.pallas import tpu as pltpu
from jax.sharding import PartitionSpec as P

INNER = 4
MESH = pl.DeviceIdType.MESH
LANES = 128
QUAD_INDEX = ((0, 1, 2), (1, 3, 4), (2, 4, 5))
BOND_K = 0.3
ANGLE_K = 4.0
ANGLE_REST = -0.33
TORSION_K = 2.0
OUTER_DT = 0.2


def dot3(left, right):
    return left[0] * right[0] + left[1] * right[1] + left[2] * right[2]


def matvec(quad, vec):
    return [dot3([quad[QUAD_INDEX[a][b]] for b in range(3)], vec) for a in range(3)]


def my_place():
    n_rep = lax.axis_size("rep")
    n_sub = lax.axis_size("sub")
    return (lax.axis_index("blk") * n_rep + lax.axis_index("rep")) * n_sub + lax.axis_index("sub")


def device_at(place):
    n_rep = lax.axis_size("rep")
    n_sub = lax.axis_size("sub")
    return (
        lax.axis_index("groups"),
        place // (n_rep * n_sub),
        (place // n_sub) % n_rep,
        place % n_sub,
    )


def greet(half, place, count):
    barrier = pltpu.get_barrier_semaphore()

    def one(j, _):
        for other in ((place + j) % count, (place + count - j) % count):
            pl.semaphore_signal(
                barrier, inc=1, device_id=device_at(other), device_id_type=MESH
            )
        return 0

    lax.fori_loop(1, half + 1, one, 0)


def all_here(half):
    pl.semaphore_wait(pltpu.get_barrier_semaphore(), 2 * half)


GROUPS = ("A1", "A2", "B1", "B2", "C1", "C2", "D1", "D2", "D3")
USED = (
    ("A1",),
    ("B1",),
    ("A1", "A2"),
    ("B1", "B2"),
    ("B1", "C1"),
    ("B1", "B2", "C1", "C2"),
    ("B1", "B2", "D1", "D2", "D3"),
)
SPLIT_LEFT = (0, 0, 0, 1, 1, 2)
SPLIT_RIGHT = (0, 1, 2, 0, 1, 0)
FIELD_K = tuple(48 * len(used) for used in USED)
FIELD_AT = tuple(sum(-(-k // LANES) * LANES for k in FIELD_K[:f]) for f in range(8))
SUM_USED = USED + (("A1",),)
SUM_AT = tuple(8 * sum(len(used) for used in SUM_USED[:f]) for f in range(9))
PAIRS = ((0, 0), (0, 1), (0, 2), (1, 1), (1, 2), (2, 2))
SRC_ROWS = tuple(-(-24 * len(used) // 16) * 16 for used in SUM_USED)
SRC_AT = tuple(sum(SRC_ROWS[:f]) for f in range(9))
SUM_SCALE = (3.0, -3.0, 3.0, 3.0, 5.0, 3.0, 3.0)


def symmetric(x, y):
    return [x[a] * y[a] if a == b else x[a] * y[b] + x[b] * y[a] for a, b in PAIRS]


def source_groups(record):
    x, c, d, q = record[0:3], record[3], record[4:7], record[7:13]
    one = jnp.ones_like(c)
    zero = jnp.zeros_like(c)
    y = matvec(q, x)
    cx = [c * v for v in x]
    cxd = [v + w for v, w in zip(cx, d)]
    xx = [x[a] * x[b] for a, b in PAIRS]
    half = [0.5 * v + w for v, w in zip(cx, d)]
    both = symmetric(half, x)
    mix = [
        2.0 * (v + w) if a == b else 2.0 * v + 4.0 * w for v, w, (a, b) in zip(both, q, PAIRS)
    ]
    outer = [x[a] * q[n] for a in range(3) for n in range(6)]
    turned = symmetric(x, y) + outer
    rows = {
        "A1": x + [one],
        "A2": xx,
        "B1": [dot3(d, x)] + d + [dot3(x, y)] + y,
        "B2": q,
        "C1": cx + [c] + cxd,
        "C2": mix,
        "D1": turned[0:8],
        "D2": turned[8:16],
        "D3": turned[16:24],
    }
    return {g: jnp.concatenate(r + [zero] * (8 - len(r)), axis=0) for g, r in rows.items()}


def target_rows(x, c, d, q):
    y = matvec(q, x)
    dx = dot3(d, x)
    xy = dot3(x, y)
    diag = [2.0 * x[a] * x[b] if a != b else x[a] * x[a] for a, b in PAIRS]
    cxd = [c * v + w for v, w in zip(x, d)]
    half = [0.5 * c * v + w for v, w in zip(x, d)]
    cross = [2.0 * v for v in symmetric(half, x)]
    turn = symmetric(y, x)
    twist = []
    for a in range(3):
        for b, e in PAIRS:
            first = q[QUAD_INDEX[a][b]] * x[e]
            twist.append(first if b == e else first + q[QUAD_INDEX[a][e]] * x[b])
    tail = [-20.0 * v for v in q] + [20.0 * v for v in twist]
    place = {"D1": 0, "D2": 8, "D3": 16}
    entries = []
    entries += [(0, "A1", a, d[a]) for a in range(3)] + [(0, "A1", 3, -dx)]
    entries += [(1, "B1", 1 + a, -x[a]) for a in range(3)]
    entries += [(2, "A1", a, -10.0 * y[a]) for a in range(3)] + [(2, "A1", 3, 5.0 * xy)]
    entries += [
        (2, "A2", n, (5.0 if a == b else 10.0) * q[n]) for n, (a, b) in enumerate(PAIRS)
    ]
    entries += [(3, "B1", 5 + a, -10.0 * x[a]) for a in range(3)]
    entries += [(3, "B2", n, 5.0 * diag[n]) for n in range(6)]
    entries += [(4, "B1", 1 + a, 0.2 * cxd[a]) for a in range(3)]
    entries += [(4, "C1", a, 0.2 * d[a]) for a in range(3)] + [(4, "C1", 3, -0.2 * dx)]
    entries += [(5, "B1", 5 + a, -2.0 * cxd[a]) for a in range(3)]
    entries += [(5, "B2", n, cross[n]) for n in range(6)]
    entries += [(5, "C1", 3, xy)] + [(5, "C1", 4 + a, -2.0 * y[a]) for a in range(3)]
    entries += [(5, "C2", n, q[n]) for n in range(6)]
    entries += [(6, "B1", 5 + a, 20.0 * y[a]) for a in range(3)]
    entries += [(6, "B2", n, -20.0 * turn[n]) for n in range(6)]
    entries += [
        (6, g, n, tail[at + n]) for g, at in place.items() for n in range(8)
    ]
    return entries


def fixed_rows(c):
    one = jnp.ones_like(c)
    return [(1, "B1", 0, one), (3, "B1", 4, 5.0 * one), (4, "B1", 0, -0.2 * c), (5, "B1", 4, c)]


def thirds(x):
    top = x.astype(jnp.bfloat16).astype(jnp.float32)
    rest = x - top
    mid = rest.astype(jnp.bfloat16).astype(jnp.float32)
    return top, mid, rest - mid


def target_matrix(record, store):
    c = record[3]
    zero = jnp.zeros_like(c)
    rows = {}
    for f, g, n, v in target_rows(record[0:3], c, record[4:7], record[7:13]) + fixed_rows(c):
        rows[f, g, n] = v
    width = c.shape[1]
    for f, used in enumerate(USED):
        parts = thirds(
            jnp.concatenate([rows.get((f, g, n), zero) for g in used for n in range(8)], axis=0)
        )
        whole = [parts[s] for s in SPLIT_LEFT]
        pad = -FIELD_K[f] % LANES
        if pad:
            whole.append(jnp.zeros((pad, width), jnp.float32))
        whole = jnp.concatenate(whole, axis=0)
        for at in range(0, whole.shape[0], LANES):
            for lane in range(0, width, LANES):
                store(
                    lane,
                    FIELD_AT[f] + at,
                    whole[at : at + LANES, lane : lane + LANES].T.astype(jnp.bfloat16),
                )


def split_groups(groups):
    return {g: thirds(x) for g, x in groups.items()}


def field_source(cut, f):
    return jnp.concatenate(
        [cut[g][s] for s in SPLIT_RIGHT for g in USED[f]], axis=0
    ).astype(jnp.bfloat16)


def sum_source(cut, f):
    rows = [cut[g][s] for s in range(3) for g in SUM_USED[f]]
    if len(rows) % 2:
        rows.append(jnp.zeros_like(rows[0]))
    one = jnp.concatenate(rows, axis=0).astype(jnp.bfloat16)
    return jnp.concatenate([one, one], axis=1)


def fold3(x, f):
    n = 8 * len(SUM_USED[f])
    return x[0:n] + x[n : 2 * n] + x[2 * n : 3 * n]


def make_fields(cut, left_ref, gen_ref):
    for f in range(7):
        gen_ref[f] = jnp.dot(
            left_ref[:, FIELD_AT[f] : FIELD_AT[f] + FIELD_K[f]],
            field_source(cut, f),
            preferred_element_type=jnp.float32,
        )


def make_weights(wide_ref, plain_ref, at, gen_ref, fld_ref, alive):
    width = gen_ref.shape[1]

    def rows16(step, _):
        base = pl.multiple_of(step * 16, 16)
        for chunk in range(width // LANES):
            lane = chunk * LANES
            src = [plain_ref[c : c + 1, pl.ds(at + lane, LANES)] for c in (0, 1, 2, 3, 13)]
            halves = []
            for h in range(2):
                rows = pl.ds(pl.multiple_of(base + 8 * h, 8), 8)
                tgt = [wide_ref[c, rows, :] for c in range(5)]
                di, dk, qi, qk, t3, z5, z7 = [
                    gen_ref[f, rows, lane : lane + LANES] for f in range(7)
                ]
                r = [src[c] - tgt[c] for c in range(3)]
                s = dot3(r, r) + tgt[4] * src[4]
                root = lax.rsqrt(s)
                inv = root * root
                root = alive(root, base + 8 * h, lane)
                b3 = root * inv
                b5 = b3 * inv
                b7 = b5 * inv
                b9 = b7 * (1.4 * inv)
                b11 = b9 * (1.8 * inv)
                p_i = qk * b7 - dk * b5
                p_k = qi * b7 + di * b5
                w_i = qk * b9 - dk * b7
                w_k = qi * b9 + di * b7
                far = qk * b11 - dk * b9
                alpha = (
                    (b3 * (tgt[3] * src[3]) + b5 * t3)
                    + (b7 * z5 + b9 * z7)
                    + (di * w_i + qi * far)
                )
                halves.append((p_i, p_k, w_i, w_k, b3, b5, b7, alpha))
            for f in range(8):
                both = jnp.concatenate([halves[0][f], halves[1][f]], axis=0)
                top = both.astype(jnp.bfloat16)
                low = (both - top.astype(jnp.float32)).astype(jnp.bfloat16)
                fld_ref[f, pl.ds(base, 16), lane : lane + LANES] = top
                fld_ref[f, pl.ds(base, 16), width + lane : width + lane + LANES] = low
        return 0

    lax.fori_loop(0, width // 16, rows16, 0)


def sums_to_rows(cut, fld_ref):
    out = []
    for f in range(8):
        out.append(
            fold3(
                lax.dot_general(
                    sum_source(cut, f),
                    fld_ref[f],
                    (((1,), (1,)), ((), ())),
                    preferred_element_type=jnp.float32,
                ),
                f,
            )
        )
    return jnp.concatenate(out, axis=0)


SWAPPED = (1, 0, 3, 2, 4, 5, 6, 7)


def sums_to_columns(own_ref, fld_ref):
    width = fld_ref.shape[1]
    out = []
    for f in range(8):
        g = SWAPPED[f]
        stacked = jnp.concatenate([fld_ref[g, :, 0:width], fld_ref[g, :, width:]], axis=0)
        out.append(
            fold3(
                jnp.dot(
                    own_ref[SRC_AT[f] : SRC_AT[f + 1], :],
                    stacked,
                    preferred_element_type=jnp.float32,
                ),
                f,
            )
        )
    return jnp.concatenate(out, axis=0)


def gradients(sums, record):
    x, c, d, q = record[0:3], record[3], record[4:7], record[7:13]

    def row(f, g, n):
        at = SUM_AT[f] + 8 * SUM_USED[f].index(g) + n
        return sums[at : at + 1]

    keys = []

    def values(x, d, q):
        entries = target_rows(x, c, d, q)
        keys.extend(e[:3] for e in entries)
        return [e[3] for e in entries]

    _, pull = jax.vjp(values, x, d, q)
    grad_x, grad_d, grad_q = pull([SUM_SCALE[f] * row(f, g, n) for f, g, n in keys])
    total = row(7, "A1", 3)
    force = [
        15.0 * (x[a] * total - row(7, "A1", a)) - grad_x[a] for a in range(3)
    ]
    return jnp.concatenate(
        force + list(grad_d) + list(grad_q) + [jnp.zeros((4, c.shape[1]), jnp.float32)], axis=0
    )


def gather_kernel(
    count,
    pos_any,
    vel_any,
    dip_any,
    quad_any,
    scal_ref,
    bond_any,
    angle_any,
    torsion_any,
    out_ref,
    both_ref,
    left_ref,
    wide_ref,
    centre_ref,
    near_ref,
    pos_ref,
    vel_ref,
    dip_ref,
    quad_ref,
    bond_ref,
    angle_ref,
    torsion_ref,
    record_ref,
    pack_ref,
    gen_ref,
    fld_ref,
    local_sem,
    send_sem,
    recv_sem,
    pack_send,
    pack_recv,
):
    half = count // 2
    width = pos_any.shape[1]
    place = my_place()
    sub = lax.axis_index("sub")
    loads = [
        pltpu.make_async_copy(src, dst, local_sem.at[n])
        for n, (src, dst) in enumerate(
            (
                (pos_any, pos_ref),
                (vel_any, vel_ref),
                (dip_any, dip_ref),
                (quad_any, quad_ref),
                (bond_any, bond_ref),
                (angle_any, angle_ref),
                (torsion_any, torsion_ref),
            )
        )
    ]
    for load in loads:
        load.start()
    greet(half, place, count)
    for load in loads:
        load.wait()

    record_ref[...] = jnp.concatenate(
        [
            pos_ref[...],
            scal_ref[0:1, :],
            dip_ref[...],
            quad_ref[...],
            scal_ref[1:2, :],
            jnp.zeros((2, width), jnp.float32),
        ],
        axis=0,
    )

    def copy(j):
        return pltpu.make_async_remote_copy(
            src_ref=record_ref,
            dst_ref=out_ref.at[:, pl.ds(pl.multiple_of(j * width, LANES), width)],
            send_sem=send_sem.at[j],
            recv_sem=recv_sem.at[j],
            device_id=device_at((place + count - j) % count),
            device_id_type=MESH,
        )

    def start(j, _):
        copy(j).start()
        return 0

    def finish_one(j, _):
        copy(j).wait()
        return 0

    def cut(ref):
        whole = ref[...].astype(jnp.float32)
        return [
            whole[row : row + 1, at : at + width]
            for row in range(whole.shape[0])
            for at in range(0, whole.shape[1], width)
        ]

    pack_ref[...] = jnp.concatenate(
        [pos_ref[...], vel_ref[...], scal_ref[2:4, :]]
        + cut(bond_ref)
        + cut(angle_ref)
        + cut(torsion_ref),
        axis=0,
    )
    out_ref[:, 0:width] = record_ref[...]
    both_ref[sub] = pack_ref[...]
    record = [record_ref[c : c + 1, :] for c in range(14)]
    for c in range(3):
        middle = jnp.sum(record[c], axis=1, keepdims=True) * (1.0 / width)
        centre_ref[c : c + 1, :] = jnp.broadcast_to(middle, (1, LANES))
        record[c] = record[c] - middle

    def store(row, lane, tile):
        left_ref[row : row + LANES, lane : lane + LANES] = tile

    target_matrix(record, store)
    for n, c in enumerate((0, 1, 2, 3, 13)):
        scale = 1.0 / 15.0 if c == 3 else 1.0
        for at in range(0, width, LANES):
            wide_ref[n, at : at + LANES, :] = jnp.broadcast_to(
                record_ref[c : c + 1, at : at + LANES] * scale, (LANES, LANES)
            ).T
    all_here(half)
    lax.fori_loop(1, half + 1, start, 0)
    swap = pltpu.make_async_remote_copy(
        src_ref=pack_ref,
        dst_ref=both_ref.at[sub],
        send_sem=pack_send,
        recv_sem=pack_recv,
        device_id=device_at(place + 1 - 2 * sub),
        device_id_type=MESH,
    )
    swap.start()
    lane = lax.broadcasted_iota(jnp.int32, (8, LANES), 1)
    sublane = lax.broadcasted_iota(jnp.int32, (8, LANES), 0)
    diff = lane - sublane

    def alive(root, row, at):
        return jnp.where(diff == row - at, 0.0, root)

    cut = split_groups(source_groups(record))
    make_fields(cut, left_ref, gen_ref)
    make_weights(wide_ref, record_ref, 0, gen_ref, fld_ref, alive)
    near_ref[...] = sums_to_rows(cut, fld_ref)
    swap.wait()
    lax.fori_loop(1, half + 1, finish_one, 0)


def pair_kernel(
    count, left_ref, wide_ref, centre_ref, near_ref, all_ref, out_ref, gen_ref, fld_ref, own_ref, sum_ref
):
    half = count // 2
    width = left_ref.shape[0]

    def record_at(at):
        record = [all_ref[c : c + 1, pl.ds(at, width)] for c in range(14)]
        for c in range(3):
            record[c] = record[c] - centre_ref[c : c + 1, 0:1]
        return record

    def everywhere(root, row, at):
        return root

    own = split_groups(source_groups(record_at(0)))
    for f in range(8):
        part = sum_source(own, f)
        own_ref[SRC_AT[f] : SRC_AT[f] + part.shape[0], :] = part
    sum_ref[...] = near_ref[...]

    def slot(j, _):
        at = pl.multiple_of(j * width, LANES)
        record = record_at(at)
        cut = split_groups(source_groups(record))
        make_fields(cut, left_ref, gen_ref)
        make_weights(wide_ref, all_ref, at, gen_ref, fld_ref, everywhere)
        sum_ref[...] += sums_to_rows(cut, fld_ref)

        @pl.when(j < half)
        def _():
            out_ref[:, pl.ds(at, width)] = gradients(sums_to_columns(own_ref, fld_ref), record)

        return 0

    lax.fori_loop(1, half + 1, slot, 0)
    out_ref[:, 0:width] = gradients(sum_ref[...], record_at(0))


def torque_of(sums, d, q):
    field = [-sums[3 + a] for a in range(3)]
    halves = (1.0, 0.5, 0.5, 1.0, 0.5, 1.0)
    g = [halves[c] * sums[6 + c] for c in range(6)]

    def product(a, b):
        return dot3(
            [q[QUAD_INDEX[a][c]] for c in range(3)], [g[QUAD_INDEX[c][b]] for c in range(3)]
        )

    return jnp.concatenate(
        [
            d[1] * field[2] - d[2] * field[1] - 2.0 * (product(1, 2) - product(2, 1)),
            d[2] * field[0] - d[0] * field[2] - 2.0 * (product(2, 0) - product(0, 2)),
            d[0] * field[1] - d[1] * field[0] - 2.0 * (product(0, 1) - product(1, 0)),
        ],
        axis=0,
    )


def cross3(a, b):
    return [
        a[1] * b[2] - a[2] * b[1],
        a[2] * b[0] - a[0] * b[2],
        a[0] * b[1] - a[1] * b[0],
    ]


def minus(a, b):
    return [x - y for x, y in zip(a, b)]


def bond_push(first, second, rest):
    step = minus(second, first)
    sq = dot3(step, step) + 0.01
    scale = BOND_K * (1.0 - rest * lax.rsqrt(sq))
    pull = [scale * x for x in step]
    return [pull, [-x for x in pull]]


def angle_push(first, centre, third):
    a = minus(first, centre)
    b = minus(third, centre)
    ia = lax.rsqrt(dot3(a, a) + 0.01)
    ib = lax.rsqrt(dot3(b, b) + 0.01)
    cosine = dot3(a, b) * (ia * ib)
    lead = -ANGLE_K * (cosine - ANGLE_REST)
    both = lead * (ia * ib)
    on_a = lead * cosine * (ia * ia)
    on_b = lead * cosine * (ib * ib)
    fa = [both * y - on_a * x for x, y in zip(a, b)]
    fb = [both * x - on_b * y for x, y in zip(a, b)]
    return [fa, [-x - y for x, y in zip(fa, fb)], fb]


def torsion_push(p0, p1, p2, p3):
    one = minus(p1, p0)
    two = minus(p2, p1)
    three = minus(p3, p2)
    m = cross3(one, two)
    n = cross3(two, three)
    im = lax.rsqrt(dot3(m, m) + 0.1)
    in_ = lax.rsqrt(dot3(n, n) + 0.1)
    both = -TORSION_K * (im * in_)
    dih = dot3(m, n) * both
    cm = dih * (im * im)
    cn = dih * (in_ * in_)
    gm = [both * y - cm * x for x, y in zip(m, n)]
    gn = [both * x - cn * y for x, y in zip(m, n)]
    f_one = cross3(two, gm)
    f_three = cross3(gn, two)
    f_two = [x + y for x, y in zip(cross3(gm, one), cross3(three, gn))]
    return [
        [-x for x in f_one],
        minus(f_one, f_two),
        minus(f_two, f_three),
        f_three,
    ]


def split3(x):
    top = x.astype(jnp.bfloat16)
    rest = x - top.astype(jnp.float32)
    mid = rest.astype(jnp.bfloat16)
    low = (rest - mid.astype(jnp.float32)).astype(jnp.bfloat16)
    return jnp.concatenate([top, mid, low], axis=0)


def merge3(x):
    n = x.shape[0] // 3
    return x[0:n] + x[n : 2 * n] + x[2 * n : 3 * n]


def final_kernel(
    count,
    high,
    part_ref,
    both_ref,
    all_ref,
    out_ref,
    land_ref,
    force_ref,
    lo_ref,
    hi_ref,
    send_sem,
    recv_sem,
    force_send,
    force_recv,
):
    half = count // 2
    width = out_ref.shape[1]
    chunks = width // LANES
    used = 2 * chunks
    place = my_place()
    sub = lax.axis_index("sub")
    greet(half - 1, place, count)

    def copy(j):
        return pltpu.make_async_remote_copy(
            src_ref=part_ref.at[:, pl.ds(pl.multiple_of(j * width, LANES), width)],
            dst_ref=land_ref.at[j],
            send_sem=send_sem.at[j],
            recv_sem=recv_sem.at[j],
            device_id=device_at((place + j) % count),
            device_id_type=MESH,
        )

    def start(j, _):
        copy(j).start()
        return 0

    def finish_one(j, total):
        copy(j).wait()
        return total + land_ref[j]

    rows = both_ref.shape[1]
    n_mult = (rows - 10) // 7
    n_bond = 2 * width
    n_term = n_mult * n_bond
    total_terms = 2 * n_bond + 7 * n_term
    index = jnp.concatenate(
        [both_ref[k, row : row + 1, :] for row in range(8, rows) for k in range(2)], axis=1
    ).astype(jnp.int32)
    hi_part = index // LANES
    lo_part = index - hi_part * LANES
    lo_rows = lax.broadcasted_iota(jnp.int32, (LANES, total_terms), 0)
    lo_ref[...] = jnp.where(lo_rows == lo_part, 1.0, 0.0).astype(jnp.bfloat16)
    hi_rows = lax.broadcasted_iota(jnp.int32, (high, total_terms), 0)
    hi_ref[...] = jnp.where(hi_rows == hi_part, 1.0, 0.0)
    rest = jnp.concatenate([both_ref[k, 7:8, :] for k in range(2)], axis=1)
    fill = [jnp.zeros((high - used, LANES), jnp.float32)] if high > used else []

    def tiled(read, wanted):
        pieces = []
        for row in wanted:
            for k in range(2):
                for c in range(chunks):
                    pieces.append(read(k, row, c * LANES))
            pieces += fill
        return jnp.concatenate(pieces, axis=0)

    def from_pack(k, row, at):
        return both_ref[k, row : row + 1, at : at + LANES]

    def from_force(k, row, at):
        return force_ref[k, row : row + 1, at : at + LANES]

    mass = tiled(from_pack, (6, 6, 6))
    all_here(half - 1)
    lax.fori_loop(1, half, start, 0)

    def push_at(coords):
        looked = merge3(
            jnp.dot(split3(coords), lo_ref[...], preferred_element_type=jnp.float32)
        )
        hi = hi_ref[...]
        row = [
            jnp.sum(looked[c * high : (c + 1) * high] * hi, axis=0, keepdims=True)
            for c in range(3)
        ]
        cuts = [(0, n_bond), (n_bond, 2 * n_bond)]
        cuts += [(2 * n_bond + j * n_term, 2 * n_bond + (j + 1) * n_term) for j in range(7)]
        atoms = [[row[c][:, lo:up] for c in range(3)] for lo, up in cuts]
        pushes = (
            bond_push(atoms[0], atoms[1], rest)
            + angle_push(*atoms[2:5])
            + torsion_push(*atoms[5:9])
        )
        spread = jnp.concatenate(
            [jnp.concatenate([p[c] for p in pushes], axis=1) * hi for c in range(3)], axis=0
        )
        return merge3(
            lax.dot_general(
                split3(spread),
                lo_ref[...],
                (((1,), (1,)), ((), ())),
                preferred_element_type=jnp.float32,
            )
        )

    dt = OUTER_DT / INNER
    x = tiled(from_pack, (0, 1, 2))
    half_step = (0.5 * dt) * mass
    v = tiled(from_pack, (3, 4, 5)) + half_step * push_at(x)

    total = lax.fori_loop(1, half, finish_one, part_ref[:, 0:width])
    force_ref[sub] = total
    swap = pltpu.make_async_remote_copy(
        src_ref=force_ref.at[sub],
        dst_ref=force_ref.at[sub],
        send_sem=force_send,
        recv_sem=force_recv,
        device_id=device_at(place + 1 - 2 * sub),
        device_id_type=MESH,
    )
    swap.start()
    torque = torque_of(
        [total[c : c + 1] for c in range(12)],
        [all_ref[c : c + 1, 0:width] for c in range(4, 7)],
        [all_ref[c : c + 1, 0:width] for c in range(7, 13)],
    )
    swap.wait()
    v = v + (0.5 * OUTER_DT) * tiled(from_force, (0, 1, 2)) * mass

    def substep(step, carry):
        x, v = carry
        x = x + dt * v
        kick = half_step * push_at(x)
        v = v + kick
        v = v + jnp.where(step < INNER - 1, kick, 0.0)
        return x, v

    x, v = lax.fori_loop(0, INNER, substep, (x, v))

    def mine(state):
        rows = []
        for c in range(3):
            sides = [
                jnp.concatenate(
                    [
                        state[c * high + k * chunks + h : c * high + k * chunks + h + 1]
                        for h in range(chunks)
                    ],
                    axis=1,
                )
                for k in range(2)
            ]
            rows.append(jnp.where(sub == 0, sides[0], sides[1]))
        return jnp.concatenate(rows, axis=0)

    out_ref[...] = jnp.concatenate([mine(x), mine(v), total[0:3], torque], axis=0)


def body(
    positions,
    velocities,
    charges,
    dipoles,
    quadrupoles,
    damping,
    inverse_mass,
    bonds,
    bond_length,
    angles,
    torsions,
):
    atoms = positions.shape[1]
    n_sub = lax.axis_size("sub")
    count = lax.axis_size("blk") * lax.axis_size("rep") * n_sub
    slots = count // 2 + 1
    vmem = pl.BlockSpec(memory_space=pltpu.VMEM)
    dma = pltpu.SemaphoreType.DMA
    hbm = pl.BlockSpec(memory_space=pltpu.HBM)
    scalars = jnp.stack([charges, damping, inverse_mass, bond_length])
    index_rows = 2 + (angles.size + torsions.size) // atoms
    pack_rows = 8 + index_rows

    def params(**more):
        return pltpu.CompilerParams(vmem_limit_bytes=48 * 1024 * 1024, **more)

    def shape(*dims):
        return jax.ShapeDtypeStruct(dims, jnp.float32)

    everyone, both, left, wide, centre, near = pl.pallas_call(
        functools.partial(gather_kernel, count),
        out_shape=(
            shape(16, slots * atoms),
            shape(2, pack_rows, atoms),
            jax.ShapeDtypeStruct((atoms, FIELD_AT[7]), jnp.bfloat16),
            shape(5, atoms, LANES),
            shape(8, LANES),
            shape(SUM_AT[8], atoms),
        ),
        in_specs=[hbm] * 4 + [vmem] + [hbm] * 3,
        out_specs=(vmem,) * 6,
        scratch_shapes=[
            pltpu.VMEM(x.shape, x.dtype)
            for x in (positions, velocities, dipoles, quadrupoles, bonds, angles, torsions)
        ]
        + [
            pltpu.VMEM((16, atoms), jnp.float32),
            pltpu.VMEM((pack_rows, atoms), jnp.float32),
            pltpu.VMEM((7, atoms, atoms), jnp.float32),
            pltpu.VMEM((8, atoms, 2 * atoms), jnp.bfloat16),
            dma((7,)),
            dma((slots,)),
            dma((slots,)),
            dma,
            dma,
        ],
        compiler_params=params(collective_id=1),
        name="gather",
    )(positions, velocities, dipoles, quadrupoles, scalars, bonds, angles, torsions)
    parts = pl.pallas_call(
        functools.partial(pair_kernel, count),
        out_shape=shape(16, slots * atoms),
        in_specs=[vmem] * 5,
        out_specs=vmem,
        scratch_shapes=[
            pltpu.VMEM((7, atoms, atoms), jnp.float32),
            pltpu.VMEM((8, atoms, 2 * atoms), jnp.bfloat16),
            pltpu.VMEM((SRC_AT[8], 2 * atoms), jnp.bfloat16),
            pltpu.VMEM((SUM_AT[8], atoms), jnp.float32),
        ],
        compiler_params=params(),
        name="pairs",
    )(left, wide, centre, near, everyone)
    high = -(-(n_sub * atoms // LANES) // 8) * 8
    total = n_sub * index_rows * atoms
    out = pl.pallas_call(
        functools.partial(final_kernel, count, high),
        out_shape=shape(12, atoms),
        in_specs=[vmem] * 3,
        out_specs=vmem,
        scratch_shapes=[
            pltpu.VMEM((slots, 16, atoms), jnp.float32),
            pltpu.VMEM((2, 16, atoms), jnp.float32),
            pltpu.VMEM((LANES, total), jnp.bfloat16),
            pltpu.VMEM((high, total), jnp.float32),
            dma((slots,)),
            dma((slots,)),
            dma,
            dma,
        ],
        compiler_params=params(collective_id=2),
        name="finale",
    )(parts, both, everyone)
    return tuple(out[3 * n : 3 * n + 3] for n in range(4))


def solution(mesh):
    placed = (
        P(None, ("groups", "blk", "rep", "sub")),
        P(None, ("groups", "blk", "rep", "sub")),
        P(("groups", "blk", "rep", "sub")),
        P(None, ("groups", "blk", "rep", "sub")),
        P(None, ("groups", "blk", "rep", "sub")),
        P(("groups", "blk", "rep", "sub")),
        P(("groups", "blk", "rep", "sub")),
        P(None, ("groups", "blk", "rep", "sub")),
        P(("groups", "blk", "rep", "sub")),
        P(None, ("groups", "blk", "rep", "sub")),
        P(None, ("groups", "blk", "rep", "sub")),
    )
    return jax.shard_map(
        body,
        mesh=mesh,
        in_specs=placed,
        out_specs=(
            P(None, ("groups", "blk", "rep", "sub")),
            P(None, ("groups", "blk", "rep", "sub")),
            P(None, ("groups", "blk", "rep", "sub")),
            P(None, ("groups", "blk", "rep", "sub")),
        ),
        check_vma=False,
    )
```

```python
import functools

import jax
import jax.numpy as jnp
from jax import lax
from jax.experimental import pallas as pl
from jax.experimental.pallas import tpu as pltpu
from jax.sharding import PartitionSpec as P

INNER = 4
MESH = pl.DeviceIdType.MESH
LANES = 128
QUAD_INDEX = ((0, 1, 2), (1, 3, 4), (2, 4, 5))
BOND_K = 0.3
ANGLE_K = 4.0
ANGLE_REST = -0.33
TORSION_K = 2.0
OUTER_DT = 0.2


def dot3(left, right):
    return left[0] * right[0] + left[1] * right[1] + left[2] * right[2]


def matvec(quad, vec):
    return [dot3([quad[QUAD_INDEX[a][b]] for b in range(3)], vec) for a in range(3)]


def my_place():
    n_rep = lax.axis_size("rep")
    n_sub = lax.axis_size("sub")
    return (lax.axis_index("blk") * n_rep + lax.axis_index("rep")) * n_sub + lax.axis_index("sub")


def device_at(place):
    n_rep = lax.axis_size("rep")
    n_sub = lax.axis_size("sub")
    return (
        lax.axis_index("groups"),
        place // (n_rep * n_sub),
        (place // n_sub) % n_rep,
        place % n_sub,
    )


def greet(half, place, count):
    barrier = pltpu.get_barrier_semaphore()

    def one(j, _):
        for other in ((place + j) % count, (place + count - j) % count):
            pl.semaphore_signal(
                barrier, inc=1, device_id=device_at(other), device_id_type=MESH
            )
        return 0

    lax.fori_loop(1, half + 1, one, 0)


def all_here(half):
    pl.semaphore_wait(pltpu.get_barrier_semaphore(), 2 * half)


GROUPS = ("A1", "A2", "B1", "B2", "C1", "C2", "D1", "D2", "D3")
USED = (
    ("A1",),
    ("B1",),
    ("A1", "A2"),
    ("B1", "B2"),
    ("B1", "C1"),
    ("B1", "B2", "C1", "C2"),
    ("B1", "B2", "D1", "D2", "D3"),
)
SPLIT_LEFT = (0, 0, 0, 1, 1, 2)
SPLIT_RIGHT = (0, 1, 2, 0, 1, 0)
FIELD_K = tuple(48 * len(used) for used in USED)
FIELD_AT = tuple(sum(-(-k // LANES) * LANES for k in FIELD_K[:f]) for f in range(8))
SUM_USED = USED + (("A1",),)
SUM_AT = tuple(8 * sum(len(used) for used in SUM_USED[:f]) for f in range(9))
PAIRS = ((0, 0), (0, 1), (0, 2), (1, 1), (1, 2), (2, 2))
SRC_ROWS = tuple(-(-24 * len(used) // 16) * 16 for used in SUM_USED)
SRC_AT = tuple(sum(SRC_ROWS[:f]) for f in range(9))
SUM_SCALE = (3.0, -3.0, 3.0, 3.0, 5.0, 3.0, 3.0)


def symmetric(x, y):
    return [x[a] * y[a] if a == b else x[a] * y[b] + x[b] * y[a] for a, b in PAIRS]


def source_groups(record):
    x, c, d, q = record[0:3], record[3], record[4:7], record[7:13]
    one = jnp.ones_like(c)
    zero = jnp.zeros_like(c)
    y = matvec(q, x)
    cx = [c * v for v in x]
    cxd = [v + w for v, w in zip(cx, d)]
    xx = [x[a] * x[b] for a, b in PAIRS]
    half = [0.5 * v + w for v, w in zip(cx, d)]
    both = symmetric(half, x)
    mix = [
        2.0 * (v + w) if a == b else 2.0 * v + 4.0 * w for v, w, (a, b) in zip(both, q, PAIRS)
    ]
    outer = [x[a] * q[n] for a in range(3) for n in range(6)]
    turned = symmetric(x, y) + outer
    rows = {
        "A1": x + [one],
        "A2": xx,
        "B1": [dot3(d, x)] + d + [dot3(x, y)] + y,
        "B2": q,
        "C1": cx + [c] + cxd,
        "C2": mix,
        "D1": turned[0:8],
        "D2": turned[8:16],
        "D3": turned[16:24],
    }
    return {g: jnp.concatenate(r + [zero] * (8 - len(r)), axis=0) for g, r in rows.items()}


def target_rows(x, c, d, q):
    y = matvec(q, x)
    dx = dot3(d, x)
    xy = dot3(x, y)
    diag = [2.0 * x[a] * x[b] if a != b else x[a] * x[a] for a, b in PAIRS]
    cxd = [c * v + w for v, w in zip(x, d)]
    half = [0.5 * c * v + w for v, w in zip(x, d)]
    cross = [2.0 * v for v in symmetric(half, x)]
    turn = symmetric(y, x)
    twist = []
    for a in range(3):
        for b, e in PAIRS:
            first = q[QUAD_INDEX[a][b]] * x[e]
            twist.append(first if b == e else first + q[QUAD_INDEX[a][e]] * x[b])
    tail = [-20.0 * v for v in q] + [20.0 * v for v in twist]
    place = {"D1": 0, "D2": 8, "D3": 16}
    entries = []
    entries += [(0, "A1", a, d[a]) for a in range(3)] + [(0, "A1", 3, -dx)]
    entries += [(1, "B1", 1 + a, -x[a]) for a in range(3)]
    entries += [(2, "A1", a, -10.0 * y[a]) for a in range(3)] + [(2, "A1", 3, 5.0 * xy)]
    entries += [
        (2, "A2", n, (5.0 if a == b else 10.0) * q[n]) for n, (a, b) in enumerate(PAIRS)
    ]
    entries += [(3, "B1", 5 + a, -10.0 * x[a]) for a in range(3)]
    entries += [(3, "B2", n, 5.0 * diag[n]) for n in range(6)]
    entries += [(4, "B1", 1 + a, 0.2 * cxd[a]) for a in range(3)]
    entries += [(4, "C1", a, 0.2 * d[a]) for a in range(3)] + [(4, "C1", 3, -0.2 * dx)]
    entries += [(5, "B1", 5 + a, -2.0 * cxd[a]) for a in range(3)]
    entries += [(5, "B2", n, cross[n]) for n in range(6)]
    entries += [(5, "C1", 3, xy)] + [(5, "C1", 4 + a, -2.0 * y[a]) for a in range(3)]
    entries += [(5, "C2", n, q[n]) for n in range(6)]
    entries += [(6, "B1", 5 + a, 20.0 * y[a]) for a in range(3)]
    entries += [(6, "B2", n, -20.0 * turn[n]) for n in range(6)]
    entries += [
        (6, g, n, tail[at + n]) for g, at in place.items() for n in range(8)
    ]
    return entries


def fixed_rows(c):
    one = jnp.ones_like(c)
    return [(1, "B1", 0, one), (3, "B1", 4, 5.0 * one), (4, "B1", 0, -0.2 * c), (5, "B1", 4, c)]


def thirds(x):
    top = x.astype(jnp.bfloat16).astype(jnp.float32)
    rest = x - top
    mid = rest.astype(jnp.bfloat16).astype(jnp.float32)
    return top, mid, rest - mid


def target_matrix(record, store):
    c = record[3]
    zero = jnp.zeros_like(c)
    rows = {}
    for f, g, n, v in target_rows(record[0:3], c, record[4:7], record[7:13]) + fixed_rows(c):
        rows[f, g, n] = v
    width = c.shape[1]
    for f, used in enumerate(USED):
        parts = thirds(
            jnp.concatenate([rows.get((f, g, n), zero) for g in used for n in range(8)], axis=0)
        )
        whole = [parts[s] for s in SPLIT_LEFT]
        pad = -FIELD_K[f] % LANES
        if pad:
            whole.append(jnp.zeros((pad, width), jnp.float32))
        whole = jnp.concatenate(whole, axis=0)
        for at in range(0, whole.shape[0], LANES):
            for lane in range(0, width, LANES):
                store(
                    (FIELD_AT[f] + at) // LANES,
                    lane,
                    whole[at : at + LANES, lane : lane + LANES].T.astype(jnp.bfloat16),
                )


def split_groups(groups):
    return {g: thirds(x) for g, x in groups.items()}


def field_source(cut, f):
    return jnp.concatenate(
        [cut[g][s] for s in SPLIT_RIGHT for g in USED[f]], axis=0
    ).astype(jnp.bfloat16)


def sum_source(cut, f):
    rows = [cut[g][s] for s in range(3) for g in SUM_USED[f]]
    if len(rows) % 2:
        rows.append(jnp.zeros_like(rows[0]))
    one = jnp.concatenate(rows, axis=0).astype(jnp.bfloat16)
    return jnp.concatenate([one, one], axis=1)


def fold3(x, f):
    n = 8 * len(SUM_USED[f])
    return x[0:n] + x[n : 2 * n] + x[2 * n : 3 * n]


def left_rows(left_ref, f):
    first, last = FIELD_AT[f] // LANES, FIELD_AT[f + 1] // LANES
    return jnp.concatenate([left_ref[t] for t in range(first, last)], axis=1)[:, : FIELD_K[f]]


def make_fields(cut, left_ref, gen_ref):
    for f in range(7):
        gen_ref[f] = jnp.dot(
            left_rows(left_ref, f),
            field_source(cut, f),
            preferred_element_type=jnp.float32,
        )


def make_weights(wide_ref, plain_ref, at, gen_ref, fld_ref, alive):
    width = gen_ref.shape[1]

    def rows16(step, _):
        base = pl.multiple_of(step * 16, 16)
        for chunk in range(width // LANES):
            lane = chunk * LANES
            src = [plain_ref[c : c + 1, pl.ds(at + lane, LANES)] for c in (0, 1, 2, 3, 13)]
            halves = []
            for h in range(2):
                rows = pl.ds(pl.multiple_of(base + 8 * h, 8), 8)
                tgt = [wide_ref[c, rows, :] for c in range(5)]
                di, dk, qi, qk, t3, z5, z7 = [
                    gen_ref[f, rows, lane : lane + LANES] for f in range(7)
                ]
                r = [src[c] - tgt[c] for c in range(3)]
                s = dot3(r, r) + tgt[4] * src[4]
                root = lax.rsqrt(s)
                inv = root * root
                root = alive(root, base + 8 * h, lane)
                b3 = root * inv
                b5 = b3 * inv
                b7 = b5 * inv
                b9 = b7 * (1.4 * inv)
                b11 = b9 * (1.8 * inv)
                p_i = qk * b7 - dk * b5
                p_k = qi * b7 + di * b5
                w_i = qk * b9 - dk * b7
                w_k = qi * b9 + di * b7
                far = qk * b11 - dk * b9
                alpha = (
                    (b3 * (tgt[3] * src[3]) + b5 * t3)
                    + (b7 * z5 + b9 * z7)
                    + (di * w_i + qi * far)
                )
                halves.append((p_i, p_k, w_i, w_k, b3, b5, b7, alpha))
            for f in range(8):
                both = jnp.concatenate([halves[0][f], halves[1][f]], axis=0)
                top = both.astype(jnp.bfloat16)
                low = (both - top.astype(jnp.float32)).astype(jnp.bfloat16)
                fld_ref[f, chunk, pl.ds(base, 16), :] = top
                fld_ref[f, width // LANES + chunk, pl.ds(base, 16), :] = low
        return 0

    lax.fori_loop(0, width // 16, rows16, 0)


def sums_to_rows(cut, fld_ref):
    out = []
    for f in range(8):
        out.append(
            fold3(
                lax.dot_general(
                    sum_source(cut, f),
                    jnp.concatenate(
                        [fld_ref[f, t] for t in range(fld_ref.shape[1])], axis=1
                    ),
                    (((1,), (1,)), ((), ())),
                    preferred_element_type=jnp.float32,
                ),
                f,
            )
        )
    return jnp.concatenate(out, axis=0)


SWAPPED = (1, 0, 3, 2, 4, 5, 6, 7)


def sums_to_columns(own_ref, fld_ref):
    half = fld_ref.shape[1] // 2
    out = []
    for f in range(8):
        g = SWAPPED[f]
        stacked = jnp.concatenate(
            [
                jnp.concatenate([fld_ref[g, h * half + t] for t in range(half)], axis=1)
                for h in range(2)
            ],
            axis=0,
        )
        out.append(
            fold3(
                jnp.dot(
                    own_ref[SRC_AT[f] : SRC_AT[f + 1], :],
                    stacked,
                    preferred_element_type=jnp.float32,
                ),
                f,
            )
        )
    return jnp.concatenate(out, axis=0)


def gradients(sums, record):
    x, c, d, q = record[0:3], record[3], record[4:7], record[7:13]

    def row(f, g, n):
        at = SUM_AT[f] + 8 * SUM_USED[f].index(g) + n
        return sums[at : at + 1]

    keys = []

    def values(x, d, q):
        entries = target_rows(x, c, d, q)
        keys.extend(e[:3] for e in entries)
        return [e[3] for e in entries]

    _, pull = jax.vjp(values, x, d, q)
    grad_x, grad_d, grad_q = pull([SUM_SCALE[f] * row(f, g, n) for f, g, n in keys])
    total = row(7, "A1", 3)
    force = [
        15.0 * (x[a] * total - row(7, "A1", a)) - grad_x[a] for a in range(3)
    ]
    return jnp.concatenate(
        force + list(grad_d) + list(grad_q) + [jnp.zeros((4, c.shape[1]), jnp.float32)], axis=0
    )


def torque_of(sums, d, q):
    field = [-sums[3 + a] for a in range(3)]
    halves = (1.0, 0.5, 0.5, 1.0, 0.5, 1.0)
    g = [halves[c] * sums[6 + c] for c in range(6)]

    def product(a, b):
        return dot3(
            [q[QUAD_INDEX[a][c]] for c in range(3)], [g[QUAD_INDEX[c][b]] for c in range(3)]
        )

    return jnp.concatenate(
        [
            d[1] * field[2] - d[2] * field[1] - 2.0 * (product(1, 2) - product(2, 1)),
            d[2] * field[0] - d[0] * field[2] - 2.0 * (product(2, 0) - product(0, 2)),
            d[0] * field[1] - d[1] * field[0] - 2.0 * (product(0, 1) - product(1, 0)),
        ],
        axis=0,
    )


def cross3(a, b):
    return [
        a[1] * b[2] - a[2] * b[1],
        a[2] * b[0] - a[0] * b[2],
        a[0] * b[1] - a[1] * b[0],
    ]


def minus(a, b):
    return [x - y for x, y in zip(a, b)]


def bond_push(first, second, rest):
    step = minus(second, first)
    sq = dot3(step, step) + 0.01
    scale = BOND_K * (1.0 - rest * lax.rsqrt(sq))
    pull = [scale * x for x in step]
    return [pull, [-x for x in pull]]


def angle_push(first, centre, third):
    a = minus(first, centre)
    b = minus(third, centre)
    ia = lax.rsqrt(dot3(a, a) + 0.01)
    ib = lax.rsqrt(dot3(b, b) + 0.01)
    cosine = dot3(a, b) * (ia * ib)
    lead = -ANGLE_K * (cosine - ANGLE_REST)
    both = lead * (ia * ib)
    on_a = lead * cosine * (ia * ia)
    on_b = lead * cosine * (ib * ib)
    fa = [both * y - on_a * x for x, y in zip(a, b)]
    fb = [both * x - on_b * y for x, y in zip(a, b)]
    return [fa, [-x - y for x, y in zip(fa, fb)], fb]


def torsion_push(p0, p1, p2, p3):
    one = minus(p1, p0)
    two = minus(p2, p1)
    three = minus(p3, p2)
    m = cross3(one, two)
    n = cross3(two, three)
    im = lax.rsqrt(dot3(m, m) + 0.1)
    in_ = lax.rsqrt(dot3(n, n) + 0.1)
    both = -TORSION_K * (im * in_)
    dih = dot3(m, n) * both
    cm = dih * (im * im)
    cn = dih * (in_ * in_)
    gm = [both * y - cm * x for x, y in zip(m, n)]
    gn = [both * x - cn * y for x, y in zip(m, n)]
    f_one = cross3(two, gm)
    f_three = cross3(gn, two)
    f_two = [x + y for x, y in zip(cross3(gm, one), cross3(three, gn))]
    return [
        [-x for x in f_one],
        minus(f_one, f_two),
        minus(f_two, f_three),
        f_three,
    ]


def split3(x):
    top = x.astype(jnp.bfloat16)
    rest = x - top.astype(jnp.float32)
    mid = rest.astype(jnp.bfloat16)
    low = (rest - mid.astype(jnp.float32)).astype(jnp.bfloat16)
    return jnp.concatenate([top, mid, low], axis=0)


def merge3(x):
    n = x.shape[0] // 3
    return x[0:n] + x[n : 2 * n] + x[2 * n : 3 * n]


def droplet_kernel(
    count,
    high,
    pos_any,
    vel_any,
    dip_any,
    quad_any,
    charge_any,
    damp_any,
    mass_any,
    rest_any,
    bond_any,
    angle_any,
    torsion_any,
    out_ref,
    all_ref,
    both_ref,
    left_ref,
    wide_ref,
    part_ref,
    pos_ref,
    vel_ref,
    dip_ref,
    quad_ref,
    bond_ref,
    angle_ref,
    torsion_ref,
    charge_ref,
    damp_ref,
    mass_ref,
    rest_ref,
    record_ref,
    pack_ref,
    gen_ref,
    fld_ref,
    own_ref,
    sum_ref,
    land_ref,
    force_ref,
    lo_ref,
    hi_ref,
    local_sem,
    send_sem,
    recv_sem,
    pack_send,
    pack_recv,
    part_send,
    part_recv,
    force_send,
    force_recv,
):
    half = count // 2
    width = pos_any.shape[1]
    place = my_place()
    sub = lax.axis_index("sub")
    loads = [
        pltpu.make_async_copy(src, dst, local_sem.at[n])
        for n, (src, dst) in enumerate(
            (
                (pos_any, pos_ref),
                (vel_any, vel_ref),
                (dip_any, dip_ref),
                (quad_any, quad_ref),
                (bond_any, bond_ref),
                (angle_any, angle_ref),
                (torsion_any, torsion_ref),
                (charge_any, charge_ref),
                (damp_any, damp_ref),
                (mass_any, mass_ref),
                (rest_any, rest_ref),
            )
        )
    ]
    for load in loads:
        load.start()
    greet(half, place, count)
    for load in loads:
        load.wait()

    def flat(ref):
        return ref[...].reshape(1, width)

    record_ref[...] = jnp.concatenate(
        [
            pos_ref[...],
            flat(charge_ref),
            dip_ref[...],
            quad_ref[...],
            flat(damp_ref),
            jnp.zeros((2, width), jnp.float32),
        ],
        axis=0,
    )

    def copy(j):
        return pltpu.make_async_remote_copy(
            src_ref=record_ref,
            dst_ref=all_ref.at[:, pl.ds(pl.multiple_of(j * width, LANES), width)],
            send_sem=send_sem.at[j],
            recv_sem=recv_sem.at[j],
            device_id=device_at((place + count - j) % count),
            device_id_type=MESH,
        )

    def start(j, _):
        copy(j).start()
        return 0

    def cut(ref):
        whole = ref[...].astype(jnp.float32)
        return [
            whole[row : row + 1, at : at + width]
            for row in range(whole.shape[0])
            for at in range(0, whole.shape[1], width)
        ]

    pack_ref[...] = jnp.concatenate(
        [pos_ref[...], vel_ref[...], flat(mass_ref), flat(rest_ref)]
        + cut(bond_ref)
        + cut(angle_ref)
        + cut(torsion_ref),
        axis=0,
    )
    all_ref[:, 0:width] = record_ref[...]
    both_ref[sub] = pack_ref[...]
    record = [record_ref[c : c + 1, :] for c in range(14)]
    centre = []
    for c in range(3):
        middle = jnp.sum(record[c], axis=1, keepdims=True) * (1.0 / width)
        centre.append(middle)
        record[c] = record[c] - middle

    def store(at, row, tile):
        left_ref[at, row : row + LANES, :] = tile

    target_matrix(record, store)
    for n, c in enumerate((0, 1, 2, 3, 13)):
        scale = 1.0 / 15.0 if c == 3 else 1.0
        for at in range(0, width, LANES):
            wide_ref[n, at : at + LANES, :] = jnp.broadcast_to(
                record_ref[c : c + 1, at : at + LANES] * scale, (LANES, LANES)
            ).T
    all_here(half)
    lax.fori_loop(1, half + 1, start, 0)
    swap = pltpu.make_async_remote_copy(
        src_ref=pack_ref,
        dst_ref=both_ref.at[sub],
        send_sem=pack_send,
        recv_sem=pack_recv,
        device_id=device_at(place + 1 - 2 * sub),
        device_id_type=MESH,
    )
    swap.start()
    lane = lax.broadcasted_iota(jnp.int32, (8, LANES), 1)
    sublane = lax.broadcasted_iota(jnp.int32, (8, LANES), 0)
    diff = lane - sublane

    def alive(root, row, at):
        return jnp.where(diff == row - at, 0.0, root)

    cut = split_groups(source_groups(record))
    make_fields(cut, left_ref, gen_ref)
    make_weights(wide_ref, record_ref, 0, gen_ref, fld_ref, alive)
    sum_ref[...] = sums_to_rows(cut, fld_ref)
    for f in range(8):
        part = sum_source(cut, f)
        own_ref[SRC_AT[f] : SRC_AT[f] + part.shape[0], :] = part

    def everywhere(root, row, at):
        return root

    def part_copy(j):
        return pltpu.make_async_remote_copy(
            src_ref=part_ref.at[j],
            dst_ref=land_ref.at[j],
            send_sem=part_send.at[j],
            recv_sem=part_recv.at[j],
            device_id=device_at((place + j) % count),
            device_id_type=MESH,
        )

    def slot(j, _):
        at = pl.multiple_of(j * width, LANES)
        copy(j).wait()
        record = [all_ref[c : c + 1, pl.ds(at, width)] for c in range(14)]
        record = [record[c] - centre[c] for c in range(3)] + record[3:]
        cut = split_groups(source_groups(record))
        make_fields(cut, left_ref, gen_ref)
        make_weights(wide_ref, all_ref, at, gen_ref, fld_ref, everywhere)
        sum_ref[...] += sums_to_rows(cut, fld_ref)

        @pl.when(j < half)
        def _():
            part_ref[j] = gradients(sums_to_columns(own_ref, fld_ref), record)
            part_copy(j).start()

        return 0

    lax.fori_loop(1, half + 1, slot, 0)
    mine = gradients(sum_ref[...], record)

    chunks = width // LANES
    used = 2 * chunks
    swap.wait()
    rows = both_ref.shape[1]
    n_mult = (rows - 10) // 7
    n_bond = 2 * width
    n_term = n_mult * n_bond
    total_terms = 2 * n_bond + 7 * n_term
    index = jnp.concatenate(
        [both_ref[k, row : row + 1, :] for row in range(8, rows) for k in range(2)], axis=1
    ).astype(jnp.int32)
    hi_part = index // LANES
    lo_part = index - hi_part * LANES
    lo_rows = lax.broadcasted_iota(jnp.int32, (LANES, total_terms), 0)
    lo_ref[...] = jnp.where(lo_rows == lo_part, 1.0, 0.0).astype(jnp.bfloat16)
    hi_rows = lax.broadcasted_iota(jnp.int32, (high, total_terms), 0)
    hi_ref[...] = jnp.where(hi_rows == hi_part, 1.0, 0.0)
    rest = jnp.concatenate([both_ref[k, 7:8, :] for k in range(2)], axis=1)
    fill = [jnp.zeros((high - used, LANES), jnp.float32)] if high > used else []

    def tiled(read, wanted):
        pieces = []
        for row in wanted:
            for k in range(2):
                for c in range(chunks):
                    pieces.append(read(k, row, c * LANES))
            pieces += fill
        return jnp.concatenate(pieces, axis=0)

    def from_pack(k, row, at):
        return both_ref[k, row : row + 1, at : at + LANES]

    def from_force(k, row, at):
        return force_ref[k, row : row + 1, at : at + LANES]

    mass = tiled(from_pack, (6, 6, 6))
    def push_at(coords):
        looked = merge3(
            jnp.dot(split3(coords), lo_ref[...], preferred_element_type=jnp.float32)
        )
        hi = hi_ref[...]
        row = [
            jnp.sum(looked[c * high : (c + 1) * high] * hi, axis=0, keepdims=True)
            for c in range(3)
        ]
        cuts = [(0, n_bond), (n_bond, 2 * n_bond)]
        cuts += [(2 * n_bond + j * n_term, 2 * n_bond + (j + 1) * n_term) for j in range(7)]
        atoms = [[row[c][:, lo:up] for c in range(3)] for lo, up in cuts]
        pushes = (
            bond_push(atoms[0], atoms[1], rest)
            + angle_push(*atoms[2:5])
            + torsion_push(*atoms[5:9])
        )
        spread = jnp.concatenate(
            [jnp.concatenate([p[c] for p in pushes], axis=1) * hi for c in range(3)], axis=0
        )
        return merge3(
            lax.dot_general(
                split3(spread),
                lo_ref[...],
                (((1,), (1,)), ((), ())),
                preferred_element_type=jnp.float32,
            )
        )

    dt = OUTER_DT / INNER
    x = tiled(from_pack, (0, 1, 2))
    half_step = (0.5 * dt) * mass
    v = tiled(from_pack, (3, 4, 5)) + half_step * push_at(x)

    def finish_one(j, total):
        part_copy(j).wait()
        return total + land_ref[j]

    total = lax.fori_loop(1, half, finish_one, mine)
    force_ref[sub] = total
    trade = pltpu.make_async_remote_copy(
        src_ref=force_ref.at[sub],
        dst_ref=force_ref.at[sub],
        send_sem=force_send,
        recv_sem=force_recv,
        device_id=device_at(place + 1 - 2 * sub),
        device_id_type=MESH,
    )
    trade.start()
    torque = torque_of(
        [total[c : c + 1] for c in range(12)],
        [record_ref[c : c + 1, :] for c in range(4, 7)],
        [record_ref[c : c + 1, :] for c in range(7, 13)],
    )
    trade.wait()
    v = v + (0.5 * OUTER_DT) * tiled(from_force, (0, 1, 2)) * mass

    def substep(step, carry):
        x, v = carry
        x = x + dt * v
        kick = half_step * push_at(x)
        v = v + kick
        v = v + jnp.where(step < INNER - 1, kick, 0.0)
        return x, v

    x, v = lax.fori_loop(0, INNER, substep, (x, v))

    def my_part(state):
        rows = []
        for c in range(3):
            sides = [
                jnp.concatenate(
                    [
                        state[c * high + k * chunks + h : c * high + k * chunks + h + 1]
                        for h in range(chunks)
                    ],
                    axis=1,
                )
                for k in range(2)
            ]
            rows.append(jnp.where(sub == 0, sides[0], sides[1]))
        return jnp.concatenate(rows, axis=0)

    out_ref[...] = jnp.concatenate([my_part(x), my_part(v), total[0:3], torque], axis=0)


def body(
    positions,
    velocities,
    charges,
    dipoles,
    quadrupoles,
    damping,
    inverse_mass,
    bonds,
    bond_length,
    angles,
    torsions,
):
    atoms = positions.shape[1]
    n_sub = lax.axis_size("sub")
    count = lax.axis_size("blk") * lax.axis_size("rep") * n_sub
    slots = count // 2 + 1
    dma = pltpu.SemaphoreType.DMA
    index_rows = 2 + (angles.size + torsions.size) // atoms
    pack_rows = 8 + index_rows

    high = -(-(n_sub * atoms // LANES) // 8) * 8
    total = n_sub * index_rows * atoms
    inputs = (
        positions,
        velocities,
        dipoles,
        quadrupoles,
        charges,
        damping,
        inverse_mass,
        bond_length,
        bonds,
        angles,
        torsions,
    )
    local = inputs[0:4] + inputs[8:11] + inputs[4:8]
    tiles = atoms // LANES
    out = pl.pallas_call(
        functools.partial(droplet_kernel, count, high),
        out_shape=jax.ShapeDtypeStruct((12, atoms), jnp.float32),
        in_specs=[pl.BlockSpec(memory_space=pltpu.HBM)] * 11,
        out_specs=pl.BlockSpec(memory_space=pltpu.VMEM),
        scratch_shapes=[
            pltpu.VMEM((16, slots * atoms), jnp.float32),
            pltpu.VMEM((2, pack_rows, atoms), jnp.float32),
            pltpu.VMEM((FIELD_AT[7] // LANES, atoms, LANES), jnp.bfloat16),
            pltpu.VMEM((5, atoms, LANES), jnp.float32),
            pltpu.VMEM((slots, 16, atoms), jnp.float32),
        ]
        + [pltpu.VMEM(x.shape, x.dtype) for x in local]
        + [
            pltpu.VMEM((16, atoms), jnp.float32),
            pltpu.VMEM((pack_rows, atoms), jnp.float32),
            pltpu.VMEM((7, atoms, atoms), jnp.float32),
            pltpu.VMEM((8, 2 * tiles, atoms, LANES), jnp.bfloat16),
            pltpu.VMEM((SRC_AT[8], 2 * atoms), jnp.bfloat16),
            pltpu.VMEM((SUM_AT[8], atoms), jnp.float32),
            pltpu.VMEM((slots, 16, atoms), jnp.float32),
            pltpu.VMEM((2, 16, atoms), jnp.float32),
            pltpu.VMEM((LANES, total), jnp.bfloat16),
            pltpu.VMEM((high, total), jnp.float32),
            dma((11,)),
            dma((slots,)),
            dma((slots,)),
            dma,
            dma,
            dma((slots,)),
            dma((slots,)),
            dma,
            dma,
        ],
        compiler_params=pltpu.CompilerParams(
            vmem_limit_bytes=60 * 1024 * 1024, collective_id=1
        ),
        name="droplet",
    )(*inputs)
    return tuple(out[3 * n : 3 * n + 3] for n in range(4))


def solution(mesh):
    placed = (
        P(None, ("groups", "blk", "rep", "sub")),
        P(None, ("groups", "blk", "rep", "sub")),
        P(("groups", "blk", "rep", "sub")),
        P(None, ("groups", "blk", "rep", "sub")),
        P(None, ("groups", "blk", "rep", "sub")),
        P(("groups", "blk", "rep", "sub")),
        P(("groups", "blk", "rep", "sub")),
        P(None, ("groups", "blk", "rep", "sub")),
        P(("groups", "blk", "rep", "sub")),
        P(None, ("groups", "blk", "rep", "sub")),
        P(None, ("groups", "blk", "rep", "sub")),
    )
    return jax.shard_map(
        body,
        mesh=mesh,
        in_specs=placed,
        out_specs=(
            P(None, ("groups", "blk", "rep", "sub")),
            P(None, ("groups", "blk", "rep", "sub")),
            P(None, ("groups", "blk", "rep", "sub")),
            P(None, ("groups", "blk", "rep", "sub")),
        ),
        check_vma=False,
    )
```

```python
import functools

import jax
import jax.numpy as jnp
from jax import lax
from jax.experimental import pallas as pl
from jax.experimental.pallas import tpu as pltpu
from jax.sharding import PartitionSpec as P

INNER = 4
MESH = pl.DeviceIdType.MESH
LANES = 128
QUAD_INDEX = ((0, 1, 2), (1, 3, 4), (2, 4, 5))
BOND_K = 0.3
ANGLE_K = 4.0
ANGLE_REST = -0.33
TORSION_K = 2.0
OUTER_DT = 0.2


def dot3(left, right):
    return left[0] * right[0] + left[1] * right[1] + left[2] * right[2]


def matvec(quad, vec):
    return [dot3([quad[QUAD_INDEX[a][b]] for b in range(3)], vec) for a in range(3)]


def my_place():
    n_rep = lax.axis_size("rep")
    n_sub = lax.axis_size("sub")
    return (lax.axis_index("blk") * n_rep + lax.axis_index("rep")) * n_sub + lax.axis_index("sub")


def device_at(place):
    n_rep = lax.axis_size("rep")
    n_sub = lax.axis_size("sub")
    return (
        lax.axis_index("groups"),
        place // (n_rep * n_sub),
        (place // n_sub) % n_rep,
        place % n_sub,
    )


def greet(half, place, count):
    barrier = pltpu.get_barrier_semaphore()

    def one(j, _):
        for other in ((place + j) % count, (place + count - j) % count):
            pl.semaphore_signal(
                barrier, inc=1, device_id=device_at(other), device_id_type=MESH
            )
        return 0

    lax.fori_loop(1, half + 1, one, 0)


def all_here(half):
    pl.semaphore_wait(pltpu.get_barrier_semaphore(), 2 * half)


GROUPS = ("A1", "A2", "B1", "B2", "C1", "C2", "D1", "D2", "D3")
USED = (
    ("A1",),
    ("B1",),
    ("A1", "A2"),
    ("B1", "B2"),
    ("B1", "C1"),
    ("B1", "B2", "C1", "C2"),
    ("B1", "B2", "D1", "D2", "D3"),
)
SPLIT_LEFT = (0, 0, 0, 1, 1, 2)
SPLIT_RIGHT = (0, 1, 2, 0, 1, 0)
FIELD_K = tuple(48 * len(used) for used in USED)
FIELD_AT = tuple(sum(-(-k // LANES) * LANES for k in FIELD_K[:f]) for f in range(8))
SUM_USED = USED + (("A1",),)
SUM_AT = tuple(8 * sum(len(used) for used in SUM_USED[:f]) for f in range(9))
PAIRS = ((0, 0), (0, 1), (0, 2), (1, 1), (1, 2), (2, 2))
SOURCE_AT = tuple(sum(FIELD_K[:f]) for f in range(8))
SUM_FROM = SOURCE_AT[0:7] + (0,)
SUM_ROWS = tuple(-(-24 * len(used) // 16) * 16 for used in SUM_USED)
SUM_SCALE = (3.0, -3.0, 3.0, 3.0, 5.0, 3.0, 3.0)


def symmetric(x, y):
    return [x[a] * y[a] if a == b else x[a] * y[b] + x[b] * y[a] for a, b in PAIRS]


def source_groups(record):
    x, c, d, q = record[0:3], record[3], record[4:7], record[7:13]
    one = jnp.ones_like(c)
    zero = jnp.zeros_like(c)
    y = matvec(q, x)
    cx = [c * v for v in x]
    cxd = [v + w for v, w in zip(cx, d)]
    xx = [x[a] * x[b] for a, b in PAIRS]
    half = [0.5 * v + w for v, w in zip(cx, d)]
    both = symmetric(half, x)
    mix = [
        2.0 * (v + w) if a == b else 2.0 * v + 4.0 * w for v, w, (a, b) in zip(both, q, PAIRS)
    ]
    outer = [x[a] * q[n] for a in range(3) for n in range(6)]
    turned = symmetric(x, y) + outer
    rows = {
        "A1": x + [one],
        "A2": xx,
        "B1": [dot3(d, x)] + d + [dot3(x, y)] + y,
        "B2": q,
        "C1": cx + [c] + cxd,
        "C2": mix,
        "D1": turned[0:8],
        "D2": turned[8:16],
        "D3": turned[16:24],
    }
    return {g: jnp.concatenate(r + [zero] * (8 - len(r)), axis=0) for g, r in rows.items()}


def target_rows(x, c, d, q):
    y = matvec(q, x)
    dx = dot3(d, x)
    xy = dot3(x, y)
    diag = [2.0 * x[a] * x[b] if a != b else x[a] * x[a] for a, b in PAIRS]
    cxd = [c * v + w for v, w in zip(x, d)]
    half = [0.5 * c * v + w for v, w in zip(x, d)]
    cross = [2.0 * v for v in symmetric(half, x)]
    turn = symmetric(y, x)
    twist = []
    for a in range(3):
        for b, e in PAIRS:
            first = q[QUAD_INDEX[a][b]] * x[e]
            twist.append(first if b == e else first + q[QUAD_INDEX[a][e]] * x[b])
    tail = [-20.0 * v for v in q] + [20.0 * v for v in twist]
    place = {"D1": 0, "D2": 8, "D3": 16}
    entries = []
    entries += [(0, "A1", a, d[a]) for a in range(3)] + [(0, "A1", 3, -dx)]
    entries += [(1, "B1", 1 + a, -x[a]) for a in range(3)]
    entries += [(2, "A1", a, -10.0 * y[a]) for a in range(3)] + [(2, "A1", 3, 5.0 * xy)]
    entries += [
        (2, "A2", n, (5.0 if a == b else 10.0) * q[n]) for n, (a, b) in enumerate(PAIRS)
    ]
    entries += [(3, "B1", 5 + a, -10.0 * x[a]) for a in range(3)]
    entries += [(3, "B2", n, 5.0 * diag[n]) for n in range(6)]
    entries += [(4, "B1", 1 + a, 0.2 * cxd[a]) for a in range(3)]
    entries += [(4, "C1", a, 0.2 * d[a]) for a in range(3)] + [(4, "C1", 3, -0.2 * dx)]
    entries += [(5, "B1", 5 + a, -2.0 * cxd[a]) for a in range(3)]
    entries += [(5, "B2", n, cross[n]) for n in range(6)]
    entries += [(5, "C1", 3, xy)] + [(5, "C1", 4 + a, -2.0 * y[a]) for a in range(3)]
    entries += [(5, "C2", n, q[n]) for n in range(6)]
    entries += [(6, "B1", 5 + a, 20.0 * y[a]) for a in range(3)]
    entries += [(6, "B2", n, -20.0 * turn[n]) for n in range(6)]
    entries += [
        (6, g, n, tail[at + n]) for g, at in place.items() for n in range(8)
    ]
    return entries


def fixed_rows(c):
    one = jnp.ones_like(c)
    return [(1, "B1", 0, one), (3, "B1", 4, 5.0 * one), (4, "B1", 0, -0.2 * c), (5, "B1", 4, c)]


def thirds(x):
    top = x.astype(jnp.bfloat16).astype(jnp.float32)
    rest = x - top
    mid = rest.astype(jnp.bfloat16).astype(jnp.float32)
    return top, mid, rest - mid


def target_matrix(record, store):
    c = record[3]
    zero = jnp.zeros_like(c)
    rows = {}
    for f, g, n, v in target_rows(record[0:3], c, record[4:7], record[7:13]) + fixed_rows(c):
        rows[f, g, n] = v
    width = c.shape[1]
    for f, used in enumerate(USED):
        parts = thirds(
            jnp.concatenate([rows.get((f, g, n), zero) for g in used for n in range(8)], axis=0)
        )
        whole = [parts[s] for s in SPLIT_LEFT]
        pad = -FIELD_K[f] % LANES
        if pad:
            whole.append(jnp.zeros((pad, width), jnp.float32))
        whole = jnp.concatenate(whole, axis=0)
        for at in range(0, whole.shape[0], LANES):
            for lane in range(0, width, LANES):
                store(
                    (FIELD_AT[f] + at) // LANES,
                    lane,
                    whole[at : at + LANES, lane : lane + LANES].T.astype(jnp.bfloat16),
                )


def split_groups(groups):
    return {g: thirds(x) for g, x in groups.items()}


def field_source(cut, f):
    return jnp.concatenate(
        [cut[g][s] for s in SPLIT_RIGHT for g in USED[f]], axis=0
    ).astype(jnp.bfloat16)


def put_sources(cut, put):
    for f in range(7):
        rows = field_source(cut, f)
        for c in range(rows.shape[1] // LANES):
            put(c, SOURCE_AT[f], rows[:, c * LANES : (c + 1) * LANES])


def gated(x, token):
    if token is None:
        return x
    none = jnp.minimum(jnp.abs(token), 0.0)
    first = x[0:16, 0:LANES] + jnp.concatenate([none, none], axis=0).astype(x.dtype)
    top = jnp.concatenate([first, x[0:16, LANES:]], axis=1)
    return jnp.concatenate([top, x[16:]], axis=0)


def fold3(x, f):
    n = 8 * len(SUM_USED[f])
    return x[0:n] + x[n : 2 * n] + x[2 * n : 3 * n]


def left_rows(left_ref, f):
    first, last = FIELD_AT[f] // LANES, FIELD_AT[f + 1] // LANES
    return jnp.concatenate([left_ref[t] for t in range(first, last)], axis=1)[:, : FIELD_K[f]]


def make_field(read, left_ref, gen_ref, f, token=None):
    tiles = left_ref.shape[1] // LANES
    source = jnp.concatenate(
        [read(c, SOURCE_AT[f], FIELD_K[f]) for c in range(tiles)], axis=1
    )
    made = jnp.dot(
        left_rows(left_ref, f), gated(source, token), preferred_element_type=jnp.float32
    )
    gen_ref[f] = made
    return made[-8:, -LANES:]


def make_weights(wide_ref, plain_ref, at, gen_ref, fld_ref, alive, base, token=None):
    width = gen_ref.shape[1]
    tiles = width // LANES
    rows = [pl.ds(base + 8 * h, 8) for h in range(2)]
    targets = [[wide_ref[c, rows[h], :] for c in range(5)] for h in range(2)]
    if token is not None:
        none = jnp.minimum(jnp.abs(token), 0.0)
        targets = [t[0:4] + [t[4] + none] for t in targets]
    for chunk in range(tiles):
        lane = chunk * LANES
        src = [plain_ref[c : c + 1, pl.ds(at + lane, LANES)] for c in (0, 1, 2, 3, 13)]
        halves = []
        for h in range(2):
            tgt = targets[h]
            di, dk, qi, qk, t3, z5, z7 = [
                gen_ref[f, rows[h], lane : lane + LANES] for f in range(7)
            ]
            r = [src[c] - tgt[c] for c in range(3)]
            s = dot3(r, r) + tgt[4] * src[4]
            root = lax.rsqrt(s)
            inv = root * root
            root = alive(root, base + 8 * h, lane)
            b3 = root * inv
            b5 = b3 * inv
            b7 = b5 * inv
            b9 = b7 * (1.4 * inv)
            b11 = b9 * (1.8 * inv)
            p_i = qk * b7 - dk * b5
            p_k = qi * b7 + di * b5
            w_i = qk * b9 - dk * b7
            w_k = qi * b9 + di * b7
            far = qk * b11 - dk * b9
            alpha = (
                (b3 * (tgt[3] * src[3]) + b5 * t3)
                + (b7 * z5 + b9 * z7)
                + (di * w_i + qi * far)
            )
            halves.append((p_i, p_k, w_i, w_k, b3, b5, b7, alpha))
        for f in range(8):
            both = jnp.concatenate([halves[0][f], halves[1][f]], axis=0)
            top = both.astype(jnp.bfloat16)
            low = (both - top.astype(jnp.float32)).astype(jnp.bfloat16)
            fld_ref[f, chunk, pl.ds(base, 16), :] = top
            fld_ref[f, tiles + chunk, pl.ds(base, 16), :] = low
    return halves[1][7]


def sum_source(read, tiles, f):
    rows = jnp.concatenate(
        [read(c, SUM_FROM[f], SUM_ROWS[f]) for c in range(tiles)], axis=1
    )
    return jnp.concatenate([rows, rows], axis=1)


def sum_rows(read, fld_ref, f, token=None):
    tiles = fld_ref.shape[1]
    return lax.dot_general(
        gated(sum_source(read, tiles // 2, f), token),
        jnp.concatenate([fld_ref[f, t] for t in range(tiles)], axis=1),
        (((1,), (1,)), ((), ())),
        preferred_element_type=jnp.float32,
    )


def sum_columns(read, fld_ref, f, token=None):
    half = fld_ref.shape[1] // 2
    g = SWAPPED[f]
    stacked = jnp.concatenate(
        [
            jnp.concatenate([fld_ref[g, h * half + t] for t in range(half)], axis=1)
            for h in range(2)
        ],
        axis=0,
    )
    return jnp.dot(
        gated(sum_source(read, half, f), token), stacked, preferred_element_type=jnp.float32
    )


SWAPPED = (1, 0, 3, 2, 4, 5, 6, 7)


def gradients(sums, record):
    x, c, d, q = record[0:3], record[3], record[4:7], record[7:13]

    def row(f, g, n):
        at = SUM_AT[f] + 8 * SUM_USED[f].index(g) + n
        return sums[at : at + 1]

    keys = []

    def values(x, d, q):
        entries = target_rows(x, c, d, q)
        keys.extend(e[:3] for e in entries)
        return [e[3] for e in entries]

    _, pull = jax.vjp(values, x, d, q)
    grad_x, grad_d, grad_q = pull([SUM_SCALE[f] * row(f, g, n) for f, g, n in keys])
    total = row(7, "A1", 3)
    force = [
        15.0 * (x[a] * total - row(7, "A1", a)) - grad_x[a] for a in range(3)
    ]
    return jnp.concatenate(
        force + list(grad_d) + list(grad_q) + [jnp.zeros((4, c.shape[1]), jnp.float32)], axis=0
    )


def torque_of(sums, d, q):
    field = [-sums[3 + a] for a in range(3)]
    halves = (1.0, 0.5, 0.5, 1.0, 0.5, 1.0)
    g = [halves[c] * sums[6 + c] for c in range(6)]

    def product(a, b):
        return dot3(
            [q[QUAD_INDEX[a][c]] for c in range(3)], [g[QUAD_INDEX[c][b]] for c in range(3)]
        )

    return jnp.concatenate(
        [
            d[1] * field[2] - d[2] * field[1] - 2.0 * (product(1, 2) - product(2, 1)),
            d[2] * field[0] - d[0] * field[2] - 2.0 * (product(2, 0) - product(0, 2)),
            d[0] * field[1] - d[1] * field[0] - 2.0 * (product(0, 1) - product(1, 0)),
        ],
        axis=0,
    )


def cross3(a, b):
    return [
        a[1] * b[2] - a[2] * b[1],
        a[2] * b[0] - a[0] * b[2],
        a[0] * b[1] - a[1] * b[0],
    ]


def minus(a, b):
    return [x - y for x, y in zip(a, b)]


def bond_push(first, second, rest):
    step = minus(second, first)
    sq = dot3(step, step) + 0.01
    scale = BOND_K * (1.0 - rest * lax.rsqrt(sq))
    pull = [scale * x for x in step]
    return [pull, [-x for x in pull]]


def angle_push(first, centre, third):
    a = minus(first, centre)
    b = minus(third, centre)
    ia = lax.rsqrt(dot3(a, a) + 0.01)
    ib = lax.rsqrt(dot3(b, b) + 0.01)
    cosine = dot3(a, b) * (ia * ib)
    lead = -ANGLE_K * (cosine - ANGLE_REST)
    both = lead * (ia * ib)
    on_a = lead * cosine * (ia * ia)
    on_b = lead * cosine * (ib * ib)
    fa = [both * y - on_a * x for x, y in zip(a, b)]
    fb = [both * x - on_b * y for x, y in zip(a, b)]
    return [fa, [-x - y for x, y in zip(fa, fb)], fb]


def torsion_push(p0, p1, p2, p3):
    one = minus(p1, p0)
    two = minus(p2, p1)
    three = minus(p3, p2)
    m = cross3(one, two)
    n = cross3(two, three)
    im = lax.rsqrt(dot3(m, m) + 0.1)
    in_ = lax.rsqrt(dot3(n, n) + 0.1)
    both = -TORSION_K * (im * in_)
    dih = dot3(m, n) * both
    cm = dih * (im * im)
    cn = dih * (in_ * in_)
    gm = [both * y - cm * x for x, y in zip(m, n)]
    gn = [both * x - cn * y for x, y in zip(m, n)]
    f_one = cross3(two, gm)
    f_three = cross3(gn, two)
    f_two = [x + y for x, y in zip(cross3(gm, one), cross3(three, gn))]
    return [
        [-x for x in f_one],
        minus(f_one, f_two),
        minus(f_two, f_three),
        f_three,
    ]


def halves2(x):
    top = x.astype(jnp.bfloat16).astype(jnp.float32)
    return top, x - top


def droplet_kernel(
    count,
    high,
    pos_any,
    vel_any,
    dip_any,
    quad_any,
    charge_any,
    damp_any,
    mass_any,
    rest_any,
    bond_any,
    angle_any,
    torsion_any,
    out_ref,
    all_ref,
    both_ref,
    left_ref,
    wide_ref,
    part_ref,
    pos_ref,
    vel_ref,
    dip_ref,
    quad_ref,
    bond_ref,
    angle_ref,
    torsion_ref,
    charge_ref,
    damp_ref,
    mass_ref,
    rest_ref,
    record_ref,
    pack_ref,
    gen_even,
    gen_odd,
    fld_even,
    fld_odd,
    own_ref,
    source_ref,
    sum_ref,
    land_ref,
    force_ref,
    lo_ref,
    hi_ref,
    push_ref,
    index_ref,
    place_ref,
    local_sem,
    send_sem,
    recv_sem,
    pack_send,
    pack_recv,
    part_send,
    part_recv,
    force_send,
    force_recv,
):
    gen_refs = (gen_even, gen_odd)
    fld_refs = (fld_even, fld_odd)
    half = count // 2
    width = pos_any.shape[1]
    place = my_place()
    sub = lax.axis_index("sub")
    loads = [
        pltpu.make_async_copy(src, dst, local_sem.at[n])
        for n, (src, dst) in enumerate(
            (
                (pos_any, pos_ref),
                (vel_any, vel_ref),
                (dip_any, dip_ref),
                (quad_any, quad_ref),
                (bond_any, bond_ref),
                (angle_any, angle_ref),
                (torsion_any, torsion_ref),
                (charge_any, charge_ref),
                (damp_any, damp_ref),
                (mass_any, mass_ref),
                (rest_any, rest_ref),
            )
        )
    ]
    for load in loads:
        load.start()
    greet(half, place, count)
    for load in loads:
        load.wait()

    def flat(ref):
        return ref[...].reshape(1, width)

    record_ref[...] = jnp.concatenate(
        [
            pos_ref[...],
            flat(charge_ref),
            dip_ref[...],
            quad_ref[...],
            flat(damp_ref),
            jnp.zeros((2, width), jnp.float32),
        ],
        axis=0,
    )

    def copy(j):
        return pltpu.make_async_remote_copy(
            src_ref=record_ref,
            dst_ref=all_ref.at[:, pl.ds(pl.multiple_of(j * width, LANES), width)],
            send_sem=send_sem.at[j],
            recv_sem=recv_sem.at[j],
            device_id=device_at((place + count - j) % count),
            device_id_type=MESH,
        )

    def start(j, _):
        copy(j).start()
        return 0

    def cut(ref):
        whole = ref[...].astype(jnp.float32)
        return [
            whole[row : row + 1, at : at + width]
            for row in range(whole.shape[0])
            for at in range(0, whole.shape[1], width)
        ]

    pack_ref[...] = jnp.concatenate(
        [pos_ref[...], vel_ref[...], flat(mass_ref), flat(rest_ref)]
        + cut(bond_ref)
        + cut(angle_ref)
        + cut(torsion_ref),
        axis=0,
    )
    all_ref[:, 0:width] = record_ref[...]
    both_ref[sub] = pack_ref[...]
    record = [record_ref[c : c + 1, :] for c in range(14)]
    centre = []
    for c in range(3):
        middle = jnp.sum(record[c], axis=1, keepdims=True) * (1.0 / width)
        centre.append(middle)
        record[c] = record[c] - middle

    def store(at, row, tile):
        left_ref[at, row : row + LANES, :] = tile

    target_matrix(record, store)
    for n, c in enumerate((0, 1, 2, 3, 13)):
        scale = 1.0 / 15.0 if c == 3 else 1.0
        for at in range(0, width, LANES):
            wide_ref[n, at : at + LANES, :] = jnp.broadcast_to(
                record_ref[c : c + 1, at : at + LANES] * scale, (LANES, LANES)
            ).T
    all_here(half)
    lax.fori_loop(1, half + 1, start, 0)
    swap = pltpu.make_async_remote_copy(
        src_ref=pack_ref,
        dst_ref=both_ref.at[sub],
        send_sem=pack_send,
        recv_sem=pack_recv,
        device_id=device_at(place + 1 - 2 * sub),
        device_id_type=MESH,
    )
    swap.start()
    lane = lax.broadcasted_iota(jnp.int32, (8, LANES), 1)
    sublane = lax.broadcasted_iota(jnp.int32, (8, LANES), 0)
    diff = lane - sublane

    def alive(root, row, at):
        return jnp.where(diff == row - at, 0.0, root)

    def everywhere(root, row, at):
        return root

    def put_own(c, first, rows):
        own_ref[c, first : first + rows.shape[0], :] = rows

    def read_own(c, first, rows):
        return own_ref[c, first : first + rows, :]

    put_sources(split_groups(source_groups(record)), put_own)
    for f in range(7):
        make_field(read_own, left_ref, gen_refs[0], f)

    def near_rows(step, _):
        base = pl.multiple_of(step * 16, 16)
        make_weights(wide_ref, record_ref, 0, gen_refs[0], fld_refs[0], alive, base)
        return 0

    lax.fori_loop(0, width // 16, near_rows, 0)

    def part_copy(j):
        return pltpu.make_async_remote_copy(
            src_ref=part_ref.at[j],
            dst_ref=land_ref.at[j],
            send_sem=part_send.at[j],
            recv_sem=part_recv.at[j],
            device_id=device_at((place + j) % count),
            device_id_type=MESH,
        )

    def record_at(j):
        at = pl.multiple_of(j * width, LANES)
        record = [all_ref[c : c + 1, pl.ds(at, width)] for c in range(14)]
        return [record[c] - centre[c] for c in range(3)] + record[3:]

    def sources_of(j):
        slot = lax.rem(j, 3)

        def put(c, first, rows):
            source_ref[slot, c, first : first + rows.shape[0], :] = rows

        def read(c, first, rows):
            return source_ref[slot, c, first : first + rows, :]

        return put, read

    def step(t, parity, weights, after, columns, read_before=None):
        old_gen, new_gen = gen_refs[parity], gen_refs[1 - parity]
        new_fld, old_fld = fld_refs[parity], fld_refs[1 - parity]
        if after:
            copy(t + 1).wait()
            put, read_after = sources_of(t + 1)
            put_sources(split_groups(source_groups(record_at(t + 1))), put)
        if read_before is None:
            _, read_before = sources_of(t - 1)
        at = pl.multiple_of(t * width, LANES)
        cols = []

        def field(f):
            return lambda token: make_field(read_after, left_ref, new_gen, f, token)

        def by_rows(f):
            def run(token):
                summed = sum_rows(read_before, old_fld, f, token)
                sum_ref[SUM_AT[f] : SUM_AT[f + 1], :] += fold3(summed, f)
                return summed[0:8, -LANES:]

            return run

        def by_columns(f):
            def run(token):
                summed = sum_columns(read_own, old_fld, f, token)
                cols.append(fold3(summed, f))
                return summed[0:8, -LANES:]

            return run

        pieces = []
        for f in range(8):
            pieces += [field(f)] * (after and f < 7) + [by_rows(f)]
            pieces += [by_columns(f)] * columns
        per = width // 16 if weights else 1
        weighed, moved = [], []
        for n in range(per):
            if weights:
                token = moved[-2] if len(moved) > 1 else None
                weighed.append(
                    make_weights(
                        wide_ref, all_ref, at, old_gen, new_fld, everywhere, 16 * n, token
                    )
                )
            while len(moved) * per < (n + 1) * len(pieces):
                token = weighed[-3] if len(weighed) > 2 else None
                moved.append(pieces[len(moved)](token))
        if columns:
            part_ref[t - 1] = gradients(jnp.concatenate(cols, axis=0), record_at(t - 1))
            part_copy(t - 1).start()

    def two_steps(i, _):
        step(2 * i, 0, True, True, True)
        step(2 * i + 1, 1, True, True, True)
        return 0

    sum_ref[...] = jnp.zeros_like(sum_ref)
    copy(1).wait()
    put, read_first = sources_of(1)
    put_sources(split_groups(source_groups(record_at(1))), put)
    for f in range(7):
        make_field(read_first, left_ref, gen_refs[1], f)
    step(1, 1, True, True, False, read_own)
    lax.fori_loop(1, half // 2, two_steps, 0)
    step(half, 0, True, False, True)
    step(half + 1, 1, False, False, False)
    mine = gradients(sum_ref[...], record)

    chunks = width // LANES
    used = 2 * chunks
    swap.wait()
    rows = both_ref.shape[1]
    n_mult = (rows - 10) // 7
    n_bond = 2 * width
    n_term = n_mult * n_bond
    total_terms = 2 * n_bond + 7 * n_term
    index = jnp.concatenate(
        [both_ref[k, row : row + 1, :] for row in range(8, rows) for k in range(2)], axis=1
    )
    hi_part = jnp.floor(index * (1.0 / LANES))
    lo_part = index - hi_part * LANES
    lo_rows = lax.broadcasted_iota(jnp.int32, (LANES, LANES), 0).astype(jnp.float32)
    lo_rows = lo_rows.astype(jnp.bfloat16)
    hi_rows = lax.broadcasted_iota(jnp.int32, (high, LANES), 0).astype(jnp.float32)
    yes = jnp.ones((LANES, LANES), jnp.bfloat16)
    no = jnp.zeros((LANES, LANES), jnp.bfloat16)
    for at in range(0, total_terms, LANES):
        wanted = jnp.broadcast_to(lo_part[:, at : at + LANES], (LANES, LANES))
        lo_ref[at // LANES] = jnp.where(lo_rows == wanted.astype(jnp.bfloat16), yes, no)
        hi_ref[:, at : at + LANES] = jnp.where(
            hi_rows == hi_part[:, at : at + LANES], 1.0, 0.0
        )
    spans = [n_bond // LANES] * 2 + [n_term // LANES] * 7
    starts = [sum(spans[:n]) for n in range(9)]
    tall = [-(-n // 8) * 8 for n in spans]
    rest = jnp.concatenate(
        [both_ref[k, 7:8, at : at + LANES] for k in range(2) for at in range(0, width, LANES)]
        + [jnp.zeros((tall[0] - spans[0], LANES), jnp.float32)] * (tall[0] > spans[0]),
        axis=0,
    )
    lows = [sum(tall[:n]) for n in range(9)]
    whole = index.astype(jnp.int32)
    dense = []
    for at, span, rise in zip(starts, spans, tall):
        dense += [whole[:, (at + t) * LANES : (at + t + 1) * LANES] for t in range(span)]
        dense += [jnp.zeros((rise - span, LANES), jnp.int32)] * (rise > span)
    index_ref[...] = jnp.concatenate(dense, axis=0)
    fill = [jnp.zeros((high - used, LANES), jnp.float32)] if high > used else []

    def tiled(read, wanted):
        pieces = []
        for row in wanted:
            for k in range(2):
                for c in range(chunks):
                    pieces.append(read(k, row, c * LANES))
            pieces += fill
        return jnp.concatenate(pieces, axis=0)

    def from_pack(k, row, at):
        return both_ref[k, row : row + 1, at : at + LANES]

    def from_force(k, row, at):
        return force_ref[k, row : row + 1, at : at + LANES]

    mass = tiled(from_pack, (6, 6, 6))
    def all_lo():
        return jnp.concatenate([lo_ref[t] for t in range(total_terms // LANES)], axis=1)

    def push_at(coords):
        place_ref[...] = coords

        def at_rows(low):
            here = index_ref[low : low + 8, :]
            upper = here // LANES
            lower = here - upper * LANES
            near = [upper == h for h in range(used)]
            result = []
            for c in range(3):
                found = jnp.zeros((8, LANES), jnp.float32)
                for h in range(used):
                    line = jnp.broadcast_to(
                        place_ref[c * high + h : c * high + h + 1, :], (8, LANES)
                    )
                    got = jnp.take_along_axis(line, lower, axis=1, mode="promise_in_bounds")
                    found = jnp.where(near[h], got, found)
                result.append(found)
            return result

        atoms = []
        for low, rise in zip(lows, tall):
            pieces = [at_rows(low + n) for n in range(0, rise, 8)]
            atoms.append([jnp.concatenate([p[c] for p in pieces], axis=0) for c in range(3)])
        pushes = (
            bond_push(atoms[0], atoms[1], rest)
            + angle_push(*atoms[2:5])
            + torsion_push(*atoms[5:9])
        )
        for c in range(3):
            for n, part in enumerate(
                halves2(jnp.concatenate([p[c] for p in pushes], axis=0))
            ):
                push_ref[n, c] = part
        spread = jnp.concatenate(
            [
                jnp.concatenate(
                    [
                        push_ref[n, c, row : row + 1, :]
                        * hi_ref[:, (at + row - low) * LANES : (at + row - low + 1) * LANES]
                        for at, low, span in zip(starts, lows, spans)
                        for row in range(low, low + span)
                    ],
                    axis=1,
                )
                for n in range(2)
                for c in range(3)
            ],
            axis=0,
        ).astype(jnp.bfloat16)
        summed = lax.dot_general(
            spread, all_lo(), (((1,), (1,)), ((), ())), preferred_element_type=jnp.float32
        )
        return summed[0 : 3 * high] + summed[3 * high :]

    dt = OUTER_DT / INNER
    x = tiled(from_pack, (0, 1, 2))
    half_step = (0.5 * dt) * mass
    v = tiled(from_pack, (3, 4, 5)) + half_step * push_at(x)

    def finish_one(j, total):
        part_copy(j).wait()
        return total + land_ref[j]

    total = lax.fori_loop(1, half, finish_one, mine)
    force_ref[sub] = total
    trade = pltpu.make_async_remote_copy(
        src_ref=force_ref.at[sub],
        dst_ref=force_ref.at[sub],
        send_sem=force_send,
        recv_sem=force_recv,
        device_id=device_at(place + 1 - 2 * sub),
        device_id_type=MESH,
    )
    trade.start()
    torque = torque_of(
        [total[c : c + 1] for c in range(12)],
        [record_ref[c : c + 1, :] for c in range(4, 7)],
        [record_ref[c : c + 1, :] for c in range(7, 13)],
    )
    trade.wait()
    v = v + (0.5 * OUTER_DT) * tiled(from_force, (0, 1, 2)) * mass

    def substep(step, carry):
        x, v = carry
        x = x + dt * v
        kick = half_step * push_at(x)
        v = v + kick
        v = v + jnp.where(step < INNER - 1, kick, 0.0)
        return x, v

    x, v = lax.fori_loop(0, INNER, substep, (x, v))

    def my_part(state):
        rows = []
        for c in range(3):
            sides = [
                jnp.concatenate(
                    [
                        state[c * high + k * chunks + h : c * high + k * chunks + h + 1]
                        for h in range(chunks)
                    ],
                    axis=1,
                )
                for k in range(2)
            ]
            rows.append(jnp.where(sub == 0, sides[0], sides[1]))
        return jnp.concatenate(rows, axis=0)

    out_ref[...] = jnp.concatenate([my_part(x), my_part(v), total[0:3], torque], axis=0)


def body(
    positions,
    velocities,
    charges,
    dipoles,
    quadrupoles,
    damping,
    inverse_mass,
    bonds,
    bond_length,
    angles,
    torsions,
):
    atoms = positions.shape[1]
    n_sub = lax.axis_size("sub")
    count = lax.axis_size("blk") * lax.axis_size("rep") * n_sub
    slots = count // 2 + 1
    dma = pltpu.SemaphoreType.DMA
    index_rows = 2 + (angles.size + torsions.size) // atoms
    pack_rows = 8 + index_rows

    high = -(-(n_sub * atoms // LANES) // 8) * 8
    total = n_sub * index_rows * atoms
    n_mult = (index_rows - 2) // 7
    push_rows = sum(
        roles * -(-n_sub * terms // (8 * LANES)) * 8
        for roles, terms in ((2, atoms), (7, n_mult * atoms))
    )
    inputs = (
        positions,
        velocities,
        dipoles,
        quadrupoles,
        charges,
        damping,
        inverse_mass,
        bond_length,
        bonds,
        angles,
        torsions,
    )
    local = inputs[0:4] + inputs[8:11] + inputs[4:8]
    tiles = atoms // LANES
    out = pl.pallas_call(
        functools.partial(droplet_kernel, count, high),
        out_shape=pltpu.VMEM((12, atoms), jnp.float32),
        in_specs=[pl.BlockSpec(memory_space=pltpu.HBM)] * 11,
        out_specs=pl.BlockSpec(memory_space=pltpu.VMEM),
        scratch_shapes=[
            pltpu.VMEM((16, slots * atoms), jnp.float32),
            pltpu.VMEM((2, pack_rows, atoms), jnp.float32),
            pltpu.VMEM((FIELD_AT[7] // LANES, atoms, LANES), jnp.bfloat16),
            pltpu.VMEM((5, atoms, LANES), jnp.float32),
            pltpu.VMEM((slots, 16, atoms), jnp.float32),
        ]
        + [pltpu.VMEM(x.shape, x.dtype) for x in local]
        + [
            pltpu.VMEM((16, atoms), jnp.float32),
            pltpu.VMEM((pack_rows, atoms), jnp.float32),
            pltpu.VMEM((7, atoms, atoms), jnp.float32),
            pltpu.VMEM((7, atoms, atoms), jnp.float32),
            pltpu.VMEM((8, 2 * tiles, atoms, LANES), jnp.bfloat16),
            pltpu.VMEM((8, 2 * tiles, atoms, LANES), jnp.bfloat16),
            pltpu.VMEM((tiles, SOURCE_AT[7], LANES), jnp.bfloat16),
            pltpu.VMEM((3, tiles, SOURCE_AT[7], LANES), jnp.bfloat16),
            pltpu.VMEM((SUM_AT[8], atoms), jnp.float32),
            pltpu.VMEM((slots, 16, atoms), jnp.float32),
            pltpu.VMEM((2, 16, atoms), jnp.float32),
            pltpu.VMEM((total // LANES, LANES, LANES), jnp.bfloat16),
            pltpu.VMEM((high, total), jnp.float32),
            pltpu.VMEM((2, 3, push_rows, LANES), jnp.float32),
            pltpu.VMEM((push_rows, LANES), jnp.int32),
            pltpu.VMEM((3 * high, LANES), jnp.float32),
            dma((11,)),
            dma((slots,)),
            dma((slots,)),
            dma,
            dma,
            dma((slots,)),
            dma((slots,)),
            dma,
            dma,
        ],
        compiler_params=pltpu.CompilerParams(
            vmem_limit_bytes=60 * 1024 * 1024, collective_id=1
        ),
        name="droplet",
    )(*inputs)
    return tuple(out[3 * n : 3 * n + 3] for n in range(4))


def solution(mesh):
    placed = (
        P(None, ("groups", "blk", "rep", "sub")),
        P(None, ("groups", "blk", "rep", "sub")),
        P(("groups", "blk", "rep", "sub")),
        P(None, ("groups", "blk", "rep", "sub")),
        P(None, ("groups", "blk", "rep", "sub")),
        P(("groups", "blk", "rep", "sub")),
        P(("groups", "blk", "rep", "sub")),
        P(None, ("groups", "blk", "rep", "sub")),
        P(("groups", "blk", "rep", "sub")),
        P(None, ("groups", "blk", "rep", "sub")),
        P(None, ("groups", "blk", "rep", "sub")),
    )
    return jax.shard_map(
        body,
        mesh=mesh,
        in_specs=placed,
        out_specs=(
            P(None, ("groups", "blk", "rep", "sub")),
            P(None, ("groups", "blk", "rep", "sub")),
            P(None, ("groups", "blk", "rep", "sub")),
            P(None, ("groups", "blk", "rep", "sub")),
        ),
        check_vma=False,
    )
```

```python
import functools

import jax
import jax.numpy as jnp
from jax import lax
from jax.experimental import pallas as pl
from jax.experimental.pallas import tpu as pltpu
from jax.sharding import PartitionSpec as P

INNER = 4
MESH = pl.DeviceIdType.MESH
LANES = 128
QUAD_INDEX = ((0, 1, 2), (1, 3, 4), (2, 4, 5))
BOND_K = 0.3
ANGLE_K = 4.0
ANGLE_REST = -0.33
TORSION_K = 2.0
OUTER_DT = 0.2


def dot3(left, right):
    return left[0] * right[0] + left[1] * right[1] + left[2] * right[2]


def matvec(quad, vec):
    return [dot3([quad[QUAD_INDEX[a][b]] for b in range(3)], vec) for a in range(3)]


def my_place():
    n_rep = lax.axis_size("rep")
    n_sub = lax.axis_size("sub")
    return (lax.axis_index("blk") * n_rep + lax.axis_index("rep")) * n_sub + lax.axis_index("sub")


def device_at(place):
    n_rep = lax.axis_size("rep")
    n_sub = lax.axis_size("sub")
    return (
        lax.axis_index("groups"),
        place // (n_rep * n_sub),
        (place // n_sub) % n_rep,
        place % n_sub,
    )


def greet(half, place, count):
    barrier = pltpu.get_barrier_semaphore()

    def one(j, _):
        for other in ((place + j) % count, (place + count - j) % count):
            pl.semaphore_signal(
                barrier, inc=1, device_id=device_at(other), device_id_type=MESH
            )
        return 0

    lax.fori_loop(1, half + 1, one, 0)


def all_here(half):
    pl.semaphore_wait(pltpu.get_barrier_semaphore(), 2 * half)


GROUPS = ("A1", "A2", "B1", "B2", "C1", "C2", "D1", "D2", "D3")
USED = (
    ("A1",),
    ("B1",),
    ("A1", "A2"),
    ("B1", "B2"),
    ("B1", "C1"),
    ("B1", "B2", "C1", "C2"),
    ("B1", "B2", "D1", "D2", "D3"),
)
SPLIT_LEFT = (0, 0, 0, 1, 1, 2)
SPLIT_RIGHT = (0, 1, 2, 0, 1, 0)
FIELD_K = tuple(48 * len(used) for used in USED)
FIELD_AT = tuple(sum(-(-k // LANES) * LANES for k in FIELD_K[:f]) for f in range(8))
SUM_USED = USED + (("A1",),)
SUM_AT = tuple(8 * sum(len(used) for used in SUM_USED[:f]) for f in range(9))
PAIRS = ((0, 0), (0, 1), (0, 2), (1, 1), (1, 2), (2, 2))
SOURCE_AT = tuple(sum(FIELD_K[:f]) for f in range(8))
SUM_FROM = SOURCE_AT[0:7] + (0,)
SUM_ROWS = tuple(-(-24 * len(used) // 16) * 16 for used in SUM_USED)
SUM_SCALE = (3.0, -3.0, 3.0, 3.0, 5.0, 3.0, 3.0)


def symmetric(x, y):
    return [x[a] * y[a] if a == b else x[a] * y[b] + x[b] * y[a] for a, b in PAIRS]


def source_groups(record):
    x, c, d, q = record[0:3], record[3], record[4:7], record[7:13]
    one = jnp.ones_like(c)
    zero = jnp.zeros_like(c)
    y = matvec(q, x)
    cx = [c * v for v in x]
    cxd = [v + w for v, w in zip(cx, d)]
    xx = [x[a] * x[b] for a, b in PAIRS]
    half = [0.5 * v + w for v, w in zip(cx, d)]
    both = symmetric(half, x)
    mix = [
        2.0 * (v + w) if a == b else 2.0 * v + 4.0 * w for v, w, (a, b) in zip(both, q, PAIRS)
    ]
    outer = [x[a] * q[n] for a in range(3) for n in range(6)]
    turned = symmetric(x, y) + outer
    rows = {
        "A1": x + [one],
        "A2": xx,
        "B1": [dot3(d, x)] + d + [dot3(x, y)] + y,
        "B2": q,
        "C1": cx + [c] + cxd,
        "C2": mix,
        "D1": turned[0:8],
        "D2": turned[8:16],
        "D3": turned[16:24],
    }
    return {g: jnp.concatenate(r + [zero] * (8 - len(r)), axis=0) for g, r in rows.items()}


def target_rows(x, c, d, q):
    y = matvec(q, x)
    dx = dot3(d, x)
    xy = dot3(x, y)
    diag = [2.0 * x[a] * x[b] if a != b else x[a] * x[a] for a, b in PAIRS]
    cxd = [c * v + w for v, w in zip(x, d)]
    half = [0.5 * c * v + w for v, w in zip(x, d)]
    cross = [2.0 * v for v in symmetric(half, x)]
    turn = symmetric(y, x)
    twist = []
    for a in range(3):
        for b, e in PAIRS:
            first = q[QUAD_INDEX[a][b]] * x[e]
            twist.append(first if b == e else first + q[QUAD_INDEX[a][e]] * x[b])
    tail = [-20.0 * v for v in q] + [20.0 * v for v in twist]
    place = {"D1": 0, "D2": 8, "D3": 16}
    entries = []
    entries += [(0, "A1", a, d[a]) for a in range(3)] + [(0, "A1", 3, -dx)]
    entries += [(1, "B1", 1 + a, -x[a]) for a in range(3)]
    entries += [(2, "A1", a, -10.0 * y[a]) for a in range(3)] + [(2, "A1", 3, 5.0 * xy)]
    entries += [
        (2, "A2", n, (5.0 if a == b else 10.0) * q[n]) for n, (a, b) in enumerate(PAIRS)
    ]
    entries += [(3, "B1", 5 + a, -10.0 * x[a]) for a in range(3)]
    entries += [(3, "B2", n, 5.0 * diag[n]) for n in range(6)]
    entries += [(4, "B1", 1 + a, 0.2 * cxd[a]) for a in range(3)]
    entries += [(4, "C1", a, 0.2 * d[a]) for a in range(3)] + [(4, "C1", 3, -0.2 * dx)]
    entries += [(5, "B1", 5 + a, -2.0 * cxd[a]) for a in range(3)]
    entries += [(5, "B2", n, cross[n]) for n in range(6)]
    entries += [(5, "C1", 3, xy)] + [(5, "C1", 4 + a, -2.0 * y[a]) for a in range(3)]
    entries += [(5, "C2", n, q[n]) for n in range(6)]
    entries += [(6, "B1", 5 + a, 20.0 * y[a]) for a in range(3)]
    entries += [(6, "B2", n, -20.0 * turn[n]) for n in range(6)]
    entries += [
        (6, g, n, tail[at + n]) for g, at in place.items() for n in range(8)
    ]
    return entries


def fixed_rows(c):
    one = jnp.ones_like(c)
    return [(1, "B1", 0, one), (3, "B1", 4, 5.0 * one), (4, "B1", 0, -0.2 * c), (5, "B1", 4, c)]


def thirds(x):
    top = x.astype(jnp.bfloat16).astype(jnp.float32)
    rest = x - top
    mid = rest.astype(jnp.bfloat16).astype(jnp.float32)
    return top, mid, rest - mid


def target_matrix(record, store):
    c = record[3]
    zero = jnp.zeros_like(c)
    rows = {}
    for f, g, n, v in target_rows(record[0:3], c, record[4:7], record[7:13]) + fixed_rows(c):
        rows[f, g, n] = v
    width = c.shape[1]
    for f, used in enumerate(USED):
        parts = thirds(
            jnp.concatenate([rows.get((f, g, n), zero) for g in used for n in range(8)], axis=0)
        )
        whole = [parts[s] for s in SPLIT_LEFT]
        pad = -FIELD_K[f] % LANES
        if pad:
            whole.append(jnp.zeros((pad, width), jnp.float32))
        whole = jnp.concatenate(whole, axis=0)
        for at in range(0, whole.shape[0], LANES):
            for lane in range(0, width, LANES):
                store(
                    (FIELD_AT[f] + at) // LANES,
                    lane,
                    whole[at : at + LANES, lane : lane + LANES].T.astype(jnp.bfloat16),
                )


def split_groups(groups):
    return {g: thirds(x) for g, x in groups.items()}


def field_source(cut, f):
    return jnp.concatenate(
        [cut[g][s] for s in SPLIT_RIGHT for g in USED[f]], axis=0
    ).astype(jnp.bfloat16)


def put_sources(cut, put):
    for f in range(7):
        rows = field_source(cut, f)
        for c in range(rows.shape[1] // LANES):
            put(c, SOURCE_AT[f], rows[:, c * LANES : (c + 1) * LANES])


def gated(x, token):
    if token is None:
        return x
    none = jnp.minimum(jnp.abs(token), 0.0)
    first = x[0:16, 0:LANES] + jnp.concatenate([none, none], axis=0).astype(x.dtype)
    top = jnp.concatenate([first, x[0:16, LANES:]], axis=1)
    return jnp.concatenate([top, x[16:]], axis=0)


def fold3(x, f):
    n = 8 * len(SUM_USED[f])
    return x[0:n] + x[n : 2 * n] + x[2 * n : 3 * n]


def left_rows(left_ref, f):
    first, last = FIELD_AT[f] // LANES, FIELD_AT[f + 1] // LANES
    return jnp.concatenate([left_ref[t] for t in range(first, last)], axis=1)[:, : FIELD_K[f]]


def make_field(read, left_ref, gen_ref, f, token=None):
    tiles = left_ref.shape[1] // LANES
    source = jnp.concatenate(
        [read(c, SOURCE_AT[f], FIELD_K[f]) for c in range(tiles)], axis=1
    )
    made = jnp.dot(
        left_rows(left_ref, f), gated(source, token), preferred_element_type=jnp.float32
    )
    gen_ref[f] = made
    return made[-8:, -LANES:]


def make_weights(wide_ref, plain_ref, at, gen_ref, fld_ref, alive, base, token=None):
    width = gen_ref.shape[1]
    tiles = width // LANES
    rows = [pl.ds(base + 8 * h, 8) for h in range(2)]
    targets = [[wide_ref[c, rows[h], :] for c in range(5)] for h in range(2)]
    if token is not None:
        none = jnp.minimum(jnp.abs(token), 0.0)
        targets = [t[0:4] + [t[4] + none] for t in targets]
    for chunk in range(tiles):
        lane = chunk * LANES
        src = [plain_ref[c : c + 1, pl.ds(at + lane, LANES)] for c in (0, 1, 2, 3, 13)]
        halves = []
        for h in range(2):
            tgt = targets[h]
            di, dk, qi, qk, t3, z5, z7 = [
                gen_ref[f, rows[h], lane : lane + LANES] for f in range(7)
            ]
            r = [src[c] - tgt[c] for c in range(3)]
            s = dot3(r, r) + tgt[4] * src[4]
            root = lax.rsqrt(s)
            inv = root * root
            root = alive(root, base + 8 * h, lane)
            b3 = root * inv
            b5 = b3 * inv
            b7 = b5 * inv
            b9 = b7 * (1.4 * inv)
            b11 = b9 * (1.8 * inv)
            p_i = qk * b7 - dk * b5
            p_k = qi * b7 + di * b5
            w_i = qk * b9 - dk * b7
            w_k = qi * b9 + di * b7
            far = qk * b11 - dk * b9
            alpha = (
                (b3 * (tgt[3] * src[3]) + b5 * t3)
                + (b7 * z5 + b9 * z7)
                + (di * w_i + qi * far)
            )
            halves.append((p_i, p_k, w_i, w_k, b3, b5, b7, alpha))
        for f in range(8):
            both = jnp.concatenate([halves[0][f], halves[1][f]], axis=0)
            top = both.astype(jnp.bfloat16)
            low = (both - top.astype(jnp.float32)).astype(jnp.bfloat16)
            fld_ref[f, chunk, pl.ds(base, 16), :] = top
            fld_ref[f, tiles + chunk, pl.ds(base, 16), :] = low
    return halves[1][7]


def sum_source(read, tiles, f):
    rows = jnp.concatenate(
        [read(c, SUM_FROM[f], SUM_ROWS[f]) for c in range(tiles)], axis=1
    )
    return jnp.concatenate([rows, rows], axis=1)


def sum_rows(read, fld_ref, f, token=None):
    tiles = fld_ref.shape[1]
    return lax.dot_general(
        gated(sum_source(read, tiles // 2, f), token),
        jnp.concatenate([fld_ref[f, t] for t in range(tiles)], axis=1),
        (((1,), (1,)), ((), ())),
        preferred_element_type=jnp.float32,
    )


def sum_columns(read, fld_ref, f, token=None):
    half = fld_ref.shape[1] // 2
    g = SWAPPED[f]
    stacked = jnp.concatenate(
        [
            jnp.concatenate([fld_ref[g, h * half + t] for t in range(half)], axis=1)
            for h in range(2)
        ],
        axis=0,
    )
    return jnp.dot(
        gated(sum_source(read, half, f), token), stacked, preferred_element_type=jnp.float32
    )


SWAPPED = (1, 0, 3, 2, 4, 5, 6, 7)


def gradients(sums, record):
    x, c, d, q = record[0:3], record[3], record[4:7], record[7:13]

    def row(f, g, n):
        at = SUM_AT[f] + 8 * SUM_USED[f].index(g) + n
        return sums[at : at + 1]

    keys = []

    def values(x, d, q):
        entries = target_rows(x, c, d, q)
        keys.extend(e[:3] for e in entries)
        return [e[3] for e in entries]

    _, pull = jax.vjp(values, x, d, q)
    grad_x, grad_d, grad_q = pull([SUM_SCALE[f] * row(f, g, n) for f, g, n in keys])
    total = row(7, "A1", 3)
    force = [
        15.0 * (x[a] * total - row(7, "A1", a)) - grad_x[a] for a in range(3)
    ]
    return jnp.concatenate(
        force + list(grad_d) + list(grad_q) + [jnp.zeros((4, c.shape[1]), jnp.float32)], axis=0
    )


def torque_of(sums, d, q):
    field = [-sums[3 + a] for a in range(3)]
    halves = (1.0, 0.5, 0.5, 1.0, 0.5, 1.0)
    g = [halves[c] * sums[6 + c] for c in range(6)]

    def product(a, b):
        return dot3(
            [q[QUAD_INDEX[a][c]] for c in range(3)], [g[QUAD_INDEX[c][b]] for c in range(3)]
        )

    return jnp.concatenate(
        [
            d[1] * field[2] - d[2] * field[1] - 2.0 * (product(1, 2) - product(2, 1)),
            d[2] * field[0] - d[0] * field[2] - 2.0 * (product(2, 0) - product(0, 2)),
            d[0] * field[1] - d[1] * field[0] - 2.0 * (product(0, 1) - product(1, 0)),
        ],
        axis=0,
    )


def cross3(a, b):
    return [
        a[1] * b[2] - a[2] * b[1],
        a[2] * b[0] - a[0] * b[2],
        a[0] * b[1] - a[1] * b[0],
    ]


def minus(a, b):
    return [x - y for x, y in zip(a, b)]


def bond_push(first, second, rest):
    step = minus(second, first)
    sq = dot3(step, step) + 0.01
    scale = BOND_K * (1.0 - rest * lax.rsqrt(sq))
    pull = [scale * x for x in step]
    return [pull, [-x for x in pull]]


def angle_push(first, centre, third):
    a = minus(first, centre)
    b = minus(third, centre)
    ia = lax.rsqrt(dot3(a, a) + 0.01)
    ib = lax.rsqrt(dot3(b, b) + 0.01)
    cosine = dot3(a, b) * (ia * ib)
    lead = -ANGLE_K * (cosine - ANGLE_REST)
    both = lead * (ia * ib)
    on_a = lead * cosine * (ia * ia)
    on_b = lead * cosine * (ib * ib)
    fa = [both * y - on_a * x for x, y in zip(a, b)]
    fb = [both * x - on_b * y for x, y in zip(a, b)]
    return [fa, [-x - y for x, y in zip(fa, fb)], fb]


def torsion_push(p0, p1, p2, p3):
    one = minus(p1, p0)
    two = minus(p2, p1)
    three = minus(p3, p2)
    m = cross3(one, two)
    n = cross3(two, three)
    im = lax.rsqrt(dot3(m, m) + 0.1)
    in_ = lax.rsqrt(dot3(n, n) + 0.1)
    both = -TORSION_K * (im * in_)
    dih = dot3(m, n) * both
    cm = dih * (im * im)
    cn = dih * (in_ * in_)
    gm = [both * y - cm * x for x, y in zip(m, n)]
    gn = [both * x - cn * y for x, y in zip(m, n)]
    f_one = cross3(two, gm)
    f_three = cross3(gn, two)
    f_two = [x + y for x, y in zip(cross3(gm, one), cross3(three, gn))]
    return [
        [-x for x in f_one],
        minus(f_one, f_two),
        minus(f_two, f_three),
        f_three,
    ]


def halves2(x):
    top = x.astype(jnp.bfloat16).astype(jnp.float32)
    return top, x - top


def droplet_kernel(
    count,
    high,
    pos_any,
    vel_any,
    dip_any,
    quad_any,
    charge_any,
    damp_any,
    mass_any,
    rest_any,
    bond_any,
    angle_any,
    torsion_any,
    out_ref,
    all_ref,
    both_ref,
    left_ref,
    wide_ref,
    part_ref,
    pos_ref,
    vel_ref,
    dip_ref,
    quad_ref,
    bond_ref,
    angle_ref,
    torsion_ref,
    charge_ref,
    damp_ref,
    mass_ref,
    rest_ref,
    record_ref,
    pack_ref,
    gen_even,
    gen_odd,
    fld_even,
    fld_odd,
    own_ref,
    source_ref,
    sum_ref,
    col_even,
    col_odd,
    land_ref,
    force_ref,
    lo_ref,
    hi_ref,
    push_ref,
    index_ref,
    place_ref,
    local_sem,
    send_sem,
    recv_sem,
    pack_send,
    pack_recv,
    part_send,
    part_recv,
    force_send,
    force_recv,
):
    gen_refs = (gen_even, gen_odd)
    fld_refs = (fld_even, fld_odd)
    col_refs = (col_even, col_odd)
    half = count // 2
    width = pos_any.shape[1]
    place = my_place()
    sub = lax.axis_index("sub")
    loads = [
        pltpu.make_async_copy(src, dst, local_sem.at[n])
        for n, (src, dst) in enumerate(
            (
                (pos_any, pos_ref),
                (vel_any, vel_ref),
                (dip_any, dip_ref),
                (quad_any, quad_ref),
                (bond_any, bond_ref),
                (angle_any, angle_ref),
                (torsion_any, torsion_ref),
                (charge_any, charge_ref),
                (damp_any, damp_ref),
                (mass_any, mass_ref),
                (rest_any, rest_ref),
            )
        )
    ]
    for load in loads:
        load.start()
    greet(half, place, count)
    for load in loads:
        load.wait()

    def flat(ref):
        return ref[...].reshape(1, width)

    record_ref[...] = jnp.concatenate(
        [
            pos_ref[...],
            flat(charge_ref),
            dip_ref[...],
            quad_ref[...],
            flat(damp_ref),
            jnp.zeros((2, width), jnp.float32),
        ],
        axis=0,
    )

    def copy(j):
        return pltpu.make_async_remote_copy(
            src_ref=record_ref,
            dst_ref=all_ref.at[:, pl.ds(pl.multiple_of(j * width, LANES), width)],
            send_sem=send_sem.at[j],
            recv_sem=recv_sem.at[j],
            device_id=device_at((place + count - j) % count),
            device_id_type=MESH,
        )

    def start(j, _):
        copy(j).start()
        return 0

    def cut(ref):
        whole = ref[...].astype(jnp.float32)
        return [
            whole[row : row + 1, at : at + width]
            for row in range(whole.shape[0])
            for at in range(0, whole.shape[1], width)
        ]

    pack_ref[...] = jnp.concatenate(
        [pos_ref[...], vel_ref[...], flat(mass_ref), flat(rest_ref)]
        + cut(bond_ref)
        + cut(angle_ref)
        + cut(torsion_ref),
        axis=0,
    )
    all_ref[:, 0:width] = record_ref[...]
    both_ref[sub] = pack_ref[...]
    record = [record_ref[c : c + 1, :] for c in range(14)]
    centre = []
    for c in range(3):
        middle = jnp.sum(record[c], axis=1, keepdims=True) * (1.0 / width)
        centre.append(middle)
        record[c] = record[c] - middle

    def store(at, row, tile):
        left_ref[at, row : row + LANES, :] = tile

    target_matrix(record, store)
    for n, c in enumerate((0, 1, 2, 3, 13)):
        scale = 1.0 / 15.0 if c == 3 else 1.0
        for at in range(0, width, LANES):
            wide_ref[n, at : at + LANES, :] = jnp.broadcast_to(
                record_ref[c : c + 1, at : at + LANES] * scale, (LANES, LANES)
            ).T
    all_here(half)
    lax.fori_loop(1, half + 1, start, 0)
    swap = pltpu.make_async_remote_copy(
        src_ref=pack_ref,
        dst_ref=both_ref.at[sub],
        send_sem=pack_send,
        recv_sem=pack_recv,
        device_id=device_at(place + 1 - 2 * sub),
        device_id_type=MESH,
    )
    swap.start()
    lane = lax.broadcasted_iota(jnp.int32, (8, LANES), 1)
    sublane = lax.broadcasted_iota(jnp.int32, (8, LANES), 0)
    diff = lane - sublane

    def alive(root, row, at):
        return jnp.where(diff == row - at, 0.0, root)

    def everywhere(root, row, at):
        return root

    def put_own(c, first, rows):
        own_ref[c, first : first + rows.shape[0], :] = rows

    def read_own(c, first, rows):
        return own_ref[c, first : first + rows, :]

    put_sources(split_groups(source_groups(record)), put_own)
    for f in range(7):
        make_field(read_own, left_ref, gen_refs[0], f)

    def near_rows(step, _):
        base = pl.multiple_of(step * 16, 16)
        make_weights(wide_ref, record_ref, 0, gen_refs[0], fld_refs[0], alive, base)
        return 0

    lax.fori_loop(0, width // 16, near_rows, 0)

    def part_copy(j):
        return pltpu.make_async_remote_copy(
            src_ref=part_ref.at[j],
            dst_ref=land_ref.at[j],
            send_sem=part_send.at[j],
            recv_sem=part_recv.at[j],
            device_id=device_at((place + j) % count),
            device_id_type=MESH,
        )

    def record_at(j):
        at = pl.multiple_of(j * width, LANES)
        record = [all_ref[c : c + 1, pl.ds(at, width)] for c in range(14)]
        return [record[c] - centre[c] for c in range(3)] + record[3:]

    def sources_of(j):
        slot = lax.rem(j, 3)

        def put(c, first, rows):
            source_ref[slot, c, first : first + rows.shape[0], :] = rows

        def read(c, first, rows):
            return source_ref[slot, c, first : first + rows, :]

        return put, read

    def step(t, parity, weights, after, columns, chain, read_before=None):
        old_gen, new_gen = gen_refs[parity], gen_refs[1 - parity]
        new_fld, old_fld = fld_refs[parity], fld_refs[1 - parity]
        if after:
            copy(t + 1).wait()
            put, read_after = sources_of(t + 1)
            put_sources(split_groups(source_groups(record_at(t + 1))), put)
        if read_before is None:
            _, read_before = sources_of(t - 1)
        at = pl.multiple_of(t * width, LANES)

        def field(f):
            return lambda token: make_field(read_after, left_ref, new_gen, f, token)

        def by_rows(f):
            def run(token):
                summed = sum_rows(read_before, old_fld, f, token)
                sum_ref[SUM_AT[f] : SUM_AT[f + 1], :] += fold3(summed, f)
                return summed[0:8, -LANES:]

            return run

        def by_columns(f):
            def run(token):
                summed = sum_columns(read_own, old_fld, f, token)
                col_refs[1 - parity][SUM_AT[f] : SUM_AT[f + 1], :] = fold3(summed, f)
                return summed[0:8, -LANES:]

            return run

        def weigh(n):
            return lambda token: make_weights(
                wide_ref, all_ref, at, old_gen, new_fld, everywhere, 16 * n, token
            )

        def chained():
            part = gradients(col_refs[parity][...], record_at(t - 2))
            part_ref[t - 2] = part
            return part[0:8, 0:LANES]

        pieces = []
        for f in range(8):
            pieces += [field(f)] * (after and f < 7) + [by_rows(f)]
            pieces += [by_columns(f)] * columns
        per = width // 16 if weights else 1
        weighed, moved = [], []
        slow = None
        for n in range(per):
            if chain and n == per // 6:
                slow = chained()
            if weights:
                weighed.append(weigh(n)(moved[-2] if len(moved) > 1 else None))
            while len(moved) * per < (n + 1) * len(pieces):
                token = weighed[-3] if len(weighed) > 2 else None
                if slow is not None and weights and n == per - per // 4:
                    token, slow = slow, None
                moved.append(pieces[len(moved)](token))

    def two_steps(i, _):
        step(2 * i, 0, True, True, True, True)
        step(2 * i + 1, 1, True, True, True, True)

        @pl.when(i > 1)
        def _():
            part_copy(2 * i - 2).start()

        part_copy(2 * i - 1).start()
        return 0

    sum_ref[...] = jnp.zeros_like(sum_ref)
    col_even[...] = jnp.zeros_like(col_even)
    copy(1).wait()
    put, read_first = sources_of(1)
    put_sources(split_groups(source_groups(record_at(1))), put)
    for f in range(7):
        make_field(read_first, left_ref, gen_refs[1], f)
    step(1, 1, True, True, False, False, read_own)
    lax.fori_loop(1, half // 2, two_steps, 0)
    step(half, 0, True, False, True, True)
    part_copy(half - 2).start()
    chunks = width // LANES
    used = 2 * chunks
    swap.wait()
    rows = both_ref.shape[1]
    n_mult = (rows - 10) // 7
    n_bond = 2 * width
    n_term = n_mult * n_bond
    total_terms = 2 * n_bond + 7 * n_term
    index = jnp.concatenate(
        [both_ref[k, row : row + 1, :] for row in range(8, rows) for k in range(2)], axis=1
    )
    hi_part = jnp.floor(index * (1.0 / LANES))
    lo_part = index - hi_part * LANES
    lo_rows = lax.broadcasted_iota(jnp.int32, (LANES, LANES), 0).astype(jnp.float32)
    hi_rows = lax.broadcasted_iota(jnp.int32, (high, LANES), 0).astype(jnp.float32)

    def one_hot(at):
        lo_ref[at // LANES] = jnp.where(lo_rows == lo_part[:, at : at + LANES], 1.0, 0.0).astype(
            jnp.bfloat16
        )
        hi_ref[:, at : at + LANES] = jnp.where(hi_rows == hi_part[:, at : at + LANES], 1.0, 0.0)

    step(half + 1, 1, False, False, False, True)
    part_copy(half - 1).start()
    for at in range(0, total_terms, LANES):
        one_hot(at)
    mine = gradients(sum_ref[...], record)

    spans = [n_bond // LANES] * 2 + [n_term // LANES] * 7
    starts = [sum(spans[:n]) for n in range(9)]
    tall = [-(-n // 8) * 8 for n in spans]
    rest = jnp.concatenate(
        [both_ref[k, 7:8, at : at + LANES] for k in range(2) for at in range(0, width, LANES)]
        + [jnp.zeros((tall[0] - spans[0], LANES), jnp.float32)] * (tall[0] > spans[0]),
        axis=0,
    )
    lows = [sum(tall[:n]) for n in range(9)]
    whole = index.astype(jnp.int32)
    dense = []
    for at, span, rise in zip(starts, spans, tall):
        dense += [whole[:, (at + t) * LANES : (at + t + 1) * LANES] for t in range(span)]
        dense += [jnp.zeros((rise - span, LANES), jnp.int32)] * (rise > span)
    index_ref[...] = jnp.concatenate(dense, axis=0)
    fill = [jnp.zeros((high - used, LANES), jnp.float32)] if high > used else []

    def tiled(read, wanted):
        pieces = []
        for row in wanted:
            for k in range(2):
                for c in range(chunks):
                    pieces.append(read(k, row, c * LANES))
            pieces += fill
        return jnp.concatenate(pieces, axis=0)

    def from_pack(k, row, at):
        return both_ref[k, row : row + 1, at : at + LANES]

    def from_force(k, row, at):
        return force_ref[k, row : row + 1, at : at + LANES]

    mass = tiled(from_pack, (6, 6, 6))
    def all_lo():
        return jnp.concatenate([lo_ref[t] for t in range(total_terms // LANES)], axis=1)

    def push_at(coords):
        place_ref[...] = coords

        def at_rows(low):
            here = index_ref[low : low + 8, :]
            upper = here // LANES
            lower = here - upper * LANES
            near = [upper == h for h in range(used)]
            result = []
            for c in range(3):
                found = jnp.zeros((8, LANES), jnp.float32)
                for h in range(used):
                    line = jnp.broadcast_to(
                        place_ref[c * high + h : c * high + h + 1, :], (8, LANES)
                    )
                    got = jnp.take_along_axis(line, lower, axis=1, mode="promise_in_bounds")
                    found = jnp.where(near[h], got, found)
                result.append(found)
            return result

        atoms = []
        for low, rise in zip(lows, tall):
            pieces = [at_rows(low + n) for n in range(0, rise, 8)]
            atoms.append([jnp.concatenate([p[c] for p in pieces], axis=0) for c in range(3)])
        pushes = (
            bond_push(atoms[0], atoms[1], rest)
            + angle_push(*atoms[2:5])
            + torsion_push(*atoms[5:9])
        )
        for c in range(3):
            for n, part in enumerate(
                halves2(jnp.concatenate([p[c] for p in pushes], axis=0))
            ):
                push_ref[n, c] = part
        spread = jnp.concatenate(
            [
                jnp.concatenate(
                    [
                        push_ref[n, c, row : row + 1, :]
                        * hi_ref[:, (at + row - low) * LANES : (at + row - low + 1) * LANES]
                        for at, low, span in zip(starts, lows, spans)
                        for row in range(low, low + span)
                    ],
                    axis=1,
                )
                for n in range(2)
                for c in range(3)
            ],
            axis=0,
        ).astype(jnp.bfloat16)
        summed = lax.dot_general(
            spread, all_lo(), (((1,), (1,)), ((), ())), preferred_element_type=jnp.float32
        )
        return summed[0 : 3 * high] + summed[3 * high :]

    dt = OUTER_DT / INNER
    x = tiled(from_pack, (0, 1, 2))
    half_step = (0.5 * dt) * mass
    v = tiled(from_pack, (3, 4, 5)) + half_step * push_at(x)

    def finish_one(j, total):
        part_copy(j).wait()
        return total + land_ref[j]

    total = lax.fori_loop(1, half, finish_one, mine)
    force_ref[sub] = total
    trade = pltpu.make_async_remote_copy(
        src_ref=force_ref.at[sub],
        dst_ref=force_ref.at[sub],
        send_sem=force_send,
        recv_sem=force_recv,
        device_id=device_at(place + 1 - 2 * sub),
        device_id_type=MESH,
    )
    trade.start()
    torque = torque_of(
        [total[c : c + 1] for c in range(12)],
        [record_ref[c : c + 1, :] for c in range(4, 7)],
        [record_ref[c : c + 1, :] for c in range(7, 13)],
    )
    trade.wait()
    v = v + (0.5 * OUTER_DT) * tiled(from_force, (0, 1, 2)) * mass

    def substep(step, carry):
        x, v = carry
        x = x + dt * v
        kick = half_step * push_at(x)
        v = v + kick
        v = v + jnp.where(step < INNER - 1, kick, 0.0)
        return x, v

    x, v = lax.fori_loop(0, INNER, substep, (x, v))

    def my_part(state):
        rows = []
        for c in range(3):
            sides = [
                jnp.concatenate(
                    [
                        state[c * high + k * chunks + h : c * high + k * chunks + h + 1]
                        for h in range(chunks)
                    ],
                    axis=1,
                )
                for k in range(2)
            ]
            rows.append(jnp.where(sub == 0, sides[0], sides[1]))
        return jnp.concatenate(rows, axis=0)

    out_ref[...] = jnp.concatenate([my_part(x), my_part(v), total[0:3], torque], axis=0)


def body(
    positions,
    velocities,
    charges,
    dipoles,
    quadrupoles,
    damping,
    inverse_mass,
    bonds,
    bond_length,
    angles,
    torsions,
):
    atoms = positions.shape[1]
    n_sub = lax.axis_size("sub")
    count = lax.axis_size("blk") * lax.axis_size("rep") * n_sub
    slots = count // 2 + 1
    dma = pltpu.SemaphoreType.DMA
    index_rows = 2 + (angles.size + torsions.size) // atoms
    pack_rows = 8 + index_rows

    high = -(-(n_sub * atoms // LANES) // 8) * 8
    total = n_sub * index_rows * atoms
    n_mult = (index_rows - 2) // 7
    push_rows = sum(
        roles * -(-n_sub * terms // (8 * LANES)) * 8
        for roles, terms in ((2, atoms), (7, n_mult * atoms))
    )
    inputs = (
        positions,
        velocities,
        dipoles,
        quadrupoles,
        charges,
        damping,
        inverse_mass,
        bond_length,
        bonds,
        angles,
        torsions,
    )
    local = inputs[0:4] + inputs[8:11] + inputs[4:8]
    tiles = atoms // LANES
    out = pl.pallas_call(
        functools.partial(droplet_kernel, count, high),
        out_shape=pltpu.VMEM((12, atoms), jnp.float32),
        in_specs=[pl.BlockSpec(memory_space=pltpu.HBM)] * 11,
        out_specs=pl.BlockSpec(memory_space=pltpu.VMEM),
        scratch_shapes=[
            pltpu.VMEM((16, slots * atoms), jnp.float32),
            pltpu.VMEM((2, pack_rows, atoms), jnp.float32),
            pltpu.VMEM((FIELD_AT[7] // LANES, atoms, LANES), jnp.bfloat16),
            pltpu.VMEM((5, atoms, LANES), jnp.float32),
            pltpu.VMEM((slots, 16, atoms), jnp.float32),
        ]
        + [pltpu.VMEM(x.shape, x.dtype) for x in local]
        + [
            pltpu.VMEM((16, atoms), jnp.float32),
            pltpu.VMEM((pack_rows, atoms), jnp.float32),
            pltpu.VMEM((7, atoms, atoms), jnp.float32),
            pltpu.VMEM((7, atoms, atoms), jnp.float32),
            pltpu.VMEM((8, 2 * tiles, atoms, LANES), jnp.bfloat16),
            pltpu.VMEM((8, 2 * tiles, atoms, LANES), jnp.bfloat16),
            pltpu.VMEM((tiles, SOURCE_AT[7], LANES), jnp.bfloat16),
            pltpu.VMEM((3, tiles, SOURCE_AT[7], LANES), jnp.bfloat16),
            pltpu.VMEM((SUM_AT[8], atoms), jnp.float32),
            pltpu.VMEM((SUM_AT[8], atoms), jnp.float32),
            pltpu.VMEM((SUM_AT[8], atoms), jnp.float32),
            pltpu.VMEM((slots, 16, atoms), jnp.float32),
            pltpu.VMEM((2, 16, atoms), jnp.float32),
            pltpu.VMEM((total // LANES, LANES, LANES), jnp.bfloat16),
            pltpu.VMEM((high, total), jnp.float32),
            pltpu.VMEM((2, 3, push_rows, LANES), jnp.float32),
            pltpu.VMEM((push_rows, LANES), jnp.int32),
            pltpu.VMEM((3 * high, LANES), jnp.float32),
            dma((11,)),
            dma((slots,)),
            dma((slots,)),
            dma,
            dma,
            dma((slots,)),
            dma((slots,)),
            dma,
            dma,
        ],
        compiler_params=pltpu.CompilerParams(
            vmem_limit_bytes=60 * 1024 * 1024, collective_id=1
        ),
        name="droplet",
    )(*inputs)
    return tuple(out[3 * n : 3 * n + 3] for n in range(4))


def solution(mesh):
    placed = (
        P(None, ("groups", "blk", "rep", "sub")),
        P(None, ("groups", "blk", "rep", "sub")),
        P(("groups", "blk", "rep", "sub")),
        P(None, ("groups", "blk", "rep", "sub")),
        P(None, ("groups", "blk", "rep", "sub")),
        P(("groups", "blk", "rep", "sub")),
        P(("groups", "blk", "rep", "sub")),
        P(None, ("groups", "blk", "rep", "sub")),
        P(("groups", "blk", "rep", "sub")),
        P(None, ("groups", "blk", "rep", "sub")),
        P(None, ("groups", "blk", "rep", "sub")),
    )
    return jax.shard_map(
        body,
        mesh=mesh,
        in_specs=placed,
        out_specs=(
            P(None, ("groups", "blk", "rep", "sub")),
            P(None, ("groups", "blk", "rep", "sub")),
            P(None, ("groups", "blk", "rep", "sub")),
            P(None, ("groups", "blk", "rep", "sub")),
        ),
        check_vma=False,
    )
```
